512 devices in a mesh: sect: 4 (over z_lo, core), blk: 128 (over z_hi, x, y).
Axes of the slice: x: 4, y: 8, z: 8 (z_hi: 4, z_lo: 2; z = z_hi * 2 + z_lo), core: 2. Of those that a mesh axis runs over, the one named last changes fastest.
Arguments:
- last_perceptron_activations: bfloat16 [512, 192, 4304], P(('sect', 'blk')), may hold values from -6 to 6
- caption_reduction_matrix: bfloat16 [4304, 1152], P(None, 'blk'), may hold values from -0.09375 to 0.09375
- picture_reduction_matrix: bfloat16 [4304, 1152], P(None, 'blk'), may hold values from -0.09375 to 0.09375
- caption_offset_vector: float32 [1152], replicated, may hold values from -0.6 to 0.6
- picture_offset_vector: float32 [1152], replicated, may hold values from -0.6 to 0.6
- score_multiplier_array: float32 [1], replicated, may hold values from 4 to 16
- match_score_offset: float32 [1], replicated, may hold values from -6 to -2
- caption_match_position: int32 [384], replicated, may hold values from 0 to 383, each once
Outputs:
- text_grad: float32 [384, 4304], P('blk', 'sect')
The draws below stay inside these ranges and needn't reach their ends.
Inputs may be any that keep to these rules, and one draw needn't show every extreme that they name: `caption_match_position`: each text index appears exactly once, so every image has exactly one paired text.
All inputs are finite; a program needn't handle non-finite values.
Results may differ from the reference program's by a relative error of at most 0.013.
Values may be sent and summed in bfloat16 or wider, within the bound.
A program may use at most 128 MiB of HBM per device.

```python
import math
import jax
import jax.numpy as jnp
from jax import lax

D = 1152
FF = 4304
TXT_LEN = 64
IMG_TOK = 192
IMG_DEV = 1
TXT_DEV = 3
ROWS_DEV = 192
PAIRS = 384
N_SECT = 4
N_BLK = 128


def block_levels(stream_key, extent, shards, low, largest):
    def one(dim, parts):
        steps = jax.random.uniform(jax.random.fold_in(jax.random.fold_in(stream_key, 6), dim), (parts,), jnp.float32, low / len(shards), largest / len(shards))
        return jnp.repeat(jnp.exp(steps), extent[dim] // parts).reshape((-1,) + (1,) * (len(extent) - dim - 1))

    gain = one(*shards[0])
    for cut in shards[1:]:
        gain = gain * one(*cut)
    return gain


def bell_draw(key, shape, spread, reach, cuts=(), kind=jnp.bfloat16):
    entries = jax.random.normal(key, shape, jnp.float32) * spread
    if len(cuts) > 0:
        entries = block_levels(key, shape, cuts, -0.22, 0.18) * entries
    return jnp.clip(entries, min=-reach, max=reach).astype(kind)


def setup_inputs(seed: int = 0) -> dict:
    arg_keys = jax.random.split(jax.random.key(seed), 9)
    last_perceptron_activations = bell_draw(arg_keys[0], (N_SECT * N_BLK, ROWS_DEV, FF), 1.0, 6.0, ((0, 512),))
    caption_reduction_matrix = bell_draw(arg_keys[1], (FF, D), FF ** -0.5, 0.09375, ((1, 128),))
    picture_reduction_matrix = bell_draw(arg_keys[2], (FF, D), FF ** -0.5, 0.09375, ((1, 128),))
    caption_offset_vector = bell_draw(arg_keys[3], (D,), 0.1, 0.6, (), jnp.float32)
    picture_offset_vector = bell_draw(arg_keys[4], (D,), 0.1, 0.6, (), jnp.float32)
    score_multiplier_array = jnp.clip(jnp.exp(jax.random.uniform(arg_keys[5], (1,), jnp.float32, math.log(4.0), math.log(16.0))), 4.0, 16.0)
    match_score_offset = jnp.clip(jax.random.uniform(arg_keys[6], (1,), jnp.float32, -6.0, -2.0), -6.0, -2.0)
    caption_match_position = jax.random.permutation(arg_keys[7], PAIRS).astype(jnp.int32)
    return {"last_perceptron_activations": last_perceptron_activations, "caption_reduction_matrix": caption_reduction_matrix, "picture_reduction_matrix": picture_reduction_matrix, "caption_offset_vector": caption_offset_vector, "picture_offset_vector": picture_offset_vector, "score_multiplier_array": score_multiplier_array, "match_score_offset": match_score_offset, "caption_match_position": caption_match_position}


def unit_rows(pool):
    inv = lax.rsqrt(lax.optimization_barrier(jnp.sum(pool * pool, axis=-1, keepdims=True)) + 1e-06)
    return (pool * inv, inv)

def reference(last_perceptron_activations, caption_reduction_matrix, picture_reduction_matrix, caption_offset_vector, picture_offset_vector, score_multiplier_array, match_score_offset, caption_match_position):
    text_blocks = last_perceptron_activations[:N_BLK]
    image_blocks = last_perceptron_activations[N_BLK:]

    def text_block(hidden):
        outs = jnp.dot(hidden, caption_reduction_matrix, preferred_element_type=jnp.float32)
        return lax.optimization_barrier(jnp.mean(outs.reshape(TXT_DEV, TXT_LEN, D), axis=1))

    def image_block(hidden):
        outs = jnp.dot(hidden, picture_reduction_matrix, preferred_element_type=jnp.float32)
        return lax.optimization_barrier(jnp.mean(outs.reshape(IMG_DEV, IMG_TOK, D), axis=1))
    text_pool = lax.map(text_block, text_blocks).reshape(PAIRS, D) + caption_offset_vector
    image_pool = lax.map(image_block, image_blocks).reshape(PAIRS, D) + picture_offset_vector
    text_unit, text_inv = unit_rows(text_pool)
    image_unit, image_inv = unit_rows(image_pool)
    text_emb = text_unit.astype(jnp.bfloat16)
    image_emb = image_unit.astype(jnp.bfloat16)
    similarity_multiplier = score_multiplier_array[0]
    logits = similarity_multiplier * lax.dot_general(image_emb, text_emb, (((1,), (1,)), ((), ())), preferred_element_type=jnp.float32) + match_score_offset[0]
    label = jnp.where(caption_match_position[:, None] == jnp.arange(PAIRS, dtype=jnp.int32)[None, :], 1.0, -1.0).astype(jnp.float32)
    coef = (-label * jax.nn.sigmoid(-label * logits)).astype(jnp.bfloat16)
    acc = lax.dot_general(coef, image_emb, (((0,), (0,)), ((), ())), preferred_element_type=jnp.float32)
    grad = similarity_multiplier * acc
    grad_pool = (grad - text_unit * lax.optimization_barrier(jnp.sum(text_unit * grad, axis=-1, keepdims=True))) * text_inv
    dy = grad_pool.astype(jnp.bfloat16)
    text_grad = lax.dot_general(dy, caption_reduction_matrix, (((1,), (1,)), ((), ())), preferred_element_type=jnp.float32)
    return text_grad
```

```python
import functools

import jax
import jax.numpy as jnp
from jax import lax
from jax.experimental import pallas as pl
from jax.experimental.pallas import tpu as pltpu
from jax.sharding import Mesh
from jax.sharding import PartitionSpec as P

TXT_LEN = 64
NT = 3
K8 = 8
BF = jnp.bfloat16
F32 = jnp.float32
BLK = ("blk_0", "blk_1", "blk_2")
SECT_BLK = ("sect", "blk_0", "blk_1", "blk_2")
MESH = pl.DeviceIdType.MESH


def iota(shape, dim):
    return lax.broadcasted_iota(jnp.int32, shape, dim)


def dot_nn(a, b):
    return lax.dot_general(a, b, (((1,), (0,)), ((), ())), preferred_element_type=F32)


def dot_nt(a, b):
    return lax.dot_general(a, b, (((1,), (1,)), ((), ())), preferred_element_type=F32)


def kernel(
    dims,
    hid, wt, wi, bt, bi, mult, off, pos,
    out,
    hv, wv, wtmp, wm, wx, xpad,
    hsend, hrecv, hall,
    psend, precv, full,
    pf, tbuf, emb,
    arecv, dys, dyr, osend, orecv,
    lsem, ssem, rsem, zsem,
):
    NS, NZ, NX, NY, FF = dims
    FFQ = FF // NS
    LP = wtmp.shape[1]
    NZX = NZ * NX
    NM = NZX * K8
    NE = NZX * NY
    s = lax.axis_index("sect")
    z = lax.axis_index("blk_0")
    x = lax.axis_index("blk_1")
    y = lax.axis_index("blk_2")
    zx = z * NX + x
    blk = zx * NY + y

    sect_peers = [{"sect": lax.rem(s + d, NS)} for d in range(1, NS)]
    y_peers = [{"blk_2": lax.rem(y + d, NY)} for d in range(1, NY)]
    z_peers = [{"blk_0": lax.rem(z + d, NZ)} for d in range(1, NZ)]
    x_peers = [{"blk_1": lax.rem(x + d, NX)} for d in range(1, NX)]
    zx_peers = []
    for d in range(1, NZX):
        p = lax.rem(zx + d, NZX)
        zx_peers.append({"blk_0": p // NX, "blk_1": lax.rem(p, NX)})

    loads = [
        pltpu.make_async_copy(wi, wv.at[0], lsem.at[0]),
        pltpu.make_async_copy(wt, wv.at[1], lsem.at[1]),
        pltpu.make_async_copy(hid, hv, lsem.at[2]),
    ]
    for c in loads:
        c.start()
    barrier = pltpu.get_barrier_semaphore()
    everyone = sect_peers + y_peers + zx_peers
    for p in everyone:
        pl.semaphore_signal(barrier, inc=1, device_id=p, device_id_type=MESH)

    def send(src, dst, k, peer, recv=None):
        pltpu.make_async_remote_copy(
            src_ref=src, dst_ref=dst, send_sem=ssem.at[k],
            recv_sem=rsem.at[k] if recv is None else recv,
            device_id=peer, device_id_type=MESH,
        ).start()

    def await_bytes(ref, sem):
        pltpu.make_async_copy(ref, ref, sem).wait()

    me = x * NZ + z
    for m, b in ((0, bi), (1, bt)):
        loads[m].wait()
        w32 = wv[m].astype(F32)
        wtmp[...] = jnp.zeros_like(wtmp)
        for q in range(NS):
            @pl.when(s == q)
            def _(q=q, w32=w32):
                wtmp[:, :FFQ] = w32[:, q * FFQ:(q + 1) * FFQ]
        v = wtmp[...]
        brow = jnp.broadcast_to(b[...], (K8 + 1, b.shape[1]))
        pick = iota(brow.shape, 1) == blk * (K8 + 1) + iota(brow.shape, 0)
        bcol = jnp.sum(jnp.where(pick, brow, 0.0), axis=1, keepdims=True)
        hi = bcol.astype(BF).astype(F32)
        lo = (bcol - hi).astype(BF).astype(F32)
        lane = iota(v.shape, 1)
        v = jnp.where(lane == FFQ, hi, v)
        v = jnp.where(lane == FFQ + 1, lo, v)
        v = jnp.where(lane == FFQ + 2, bcol - hi - lo, v)
        wm[me, m] = v[:K8].astype(BF)
        wx[me, m] = v[K8:].astype(BF).astype(F32)

    rows = hv.shape[0]
    r8 = iota((8, rows), 0)
    t8 = iota((8, rows), 1)
    is_txt = s == 0
    at = (lax.shift_right_logical(t8, 6) == r8).astype(F32)
    ai = (r8 == s + (NT - 1)).astype(F32)
    f_txt = is_txt.astype(F32)
    a = (f_txt * at + (1.0 - f_txt) * ai).astype(BF)
    scale = jnp.where(is_txt, 1.0 / TXT_LEN, 1.0 / rows)
    loads[2].wait()
    hsum = dot_nn(a, hv[...]) * scale
    hsend[...] = jnp.zeros_like(hsend)
    for q in range(NS):
        hsend[q, :, :FFQ] = hsum[:, q * FFQ:(q + 1) * FFQ].astype(BF)
    hrecv[s] = hsend[s]

    NI = NZX * 8
    lane_i = iota((pos.shape[1], NI), 1)
    rho = lax.bitwise_and(lane_i, 7)
    img = (
        (NZX * NY) * jnp.where(rho < NT, rho, rho - NT)
        + lax.shift_right_logical(lane_i, 3) * NY + 2 * s + jnp.where(rho < NT, 1, 0)
    )
    sel = ((iota((pos.shape[1], NI), 0) == img) & (rho < 2 * NT)).astype(F32).astype(BF)
    pv = jnp.broadcast_to(pos[...], (8, pos.shape[1]))
    p_hi = lax.shift_right_logical(pv, 4).astype(F32).astype(BF)
    p_lo = lax.bitwise_and(pv, 15).astype(F32).astype(BF)
    posl = 16.0 * dot_nn(p_hi, sel) + dot_nn(p_lo, sel)

    pl.semaphore_wait(barrier, len(everyone))

    for d in range(1, NS):
        send(hsend.at[lax.rem(s + d, NS)], hrecv.at[s], 0, sect_peers[d - 1])
    for i in range(NZ - 1):
        send(wm.at[me], wm.at[me], 1, z_peers[i], zsem.at[2 * i])
        send(wx.at[me], wx.at[me], 2, z_peers[i], zsem.at[2 * i + 1])
    for i in range(NX - 1):
        send(wm.at[me], wm.at[me], 3, x_peers[i])
        send(wx.at[me], wx.at[me], 4, x_peers[i])
    await_bytes(hrecv.at[pl.ds(0, NS - 1)], rsem.at[0])
    hq = jnp.sum(hrecv[...].astype(F32), axis=0)
    lane = iota(hq.shape, 1)
    ones = ((lane >= FFQ) & (lane < FFQ + 3)).astype(F32) * f_txt
    hall[y] = (hq + ones).astype(BF)
    for p in y_peers:
        send(hall.at[y], hall.at[y], 5, p)
    for i in range(NZ - 1):
        zz = lax.rem(z + NZ - (i + 1), NZ)
        sl = x * NZ + zz
        await_bytes(wm.at[sl], zsem.at[2 * i])
        await_bytes(wx.at[sl], zsem.at[2 * i + 1])
        for p in x_peers:
            send(wm.at[sl], wm.at[sl], 3, p)
            send(wx.at[sl], wx.at[sl], 4, p)
    await_bytes(hall.at[pl.ds(0, NY - 1)], rsem.at[5])
    hrows = hall[...].reshape(NY * 8, LP)
    nx_in = (NX - 1) * NZ
    await_bytes(wm.at[pl.ds(0, nx_in)], rsem.at[3])
    await_bytes(wx.at[pl.ds(0, nx_in)], rsem.at[4])

    xpad[...] = jnp.zeros_like(xpad)
    parts = []
    for m in range(2):
        for j in range(NZX):
            wtmp[0:1, :] = wx[j, m]
            xpad[m, 0, j:j + 1, :] = wtmp[0:1, :]
    for m in range(2):
        ext = xpad[m, 0].astype(BF)
        pm = dot_nt(hrows, wm[:, m].reshape(NM, LP))
        pe = dot_nt(hrows, ext)
        parts.append((pm, pe))
    r64 = lax.bitwise_and(iota((NY * 8, 1), 0), 7)
    pm = jnp.where(r64 < NT, parts[1][0], parts[0][0])
    pe = jnp.where(r64 < NT, parts[1][1], parts[0][1])
    place = (iota((NZX, NE), 1) == y * NZX + iota((NZX, NE), 0)).astype(F32)
    pe = lax.dot_general(
        pe, place, (((1,), (0,)), ((), ())), preferred_element_type=F32,
        precision=lax.Precision.HIGHEST,
    )
    psend[:, :, :NM] = pm.reshape(NS, 2 * 8, NM)
    psend[:, :, NM:] = pe.reshape(NS, 2 * 8, NE)
    precv[s] = psend[s]
    for d in range(1, NS):
        send(psend.at[lax.rem(s + d, NS)], precv.at[s], 6, sect_peers[d - 1])
    await_bytes(precv.at[pl.ds(0, NS - 1)], rsem.at[6])
    full[y] = jnp.sum(precv[...], axis=0)
    for p in y_peers:
        send(full.at[y], full.at[y], 7, p)
    await_bytes(full.at[pl.ds(0, NY - 1)], rsem.at[7])
    fv = full[...]
    extra = jnp.sum(fv[:, :, NM:], axis=0)
    pool = jnp.concatenate([fv[j, :, :NM] for j in range(NY)] + [extra], axis=1)
    D = pool.shape[1]
    pf[...] = pool.reshape(2, 8, D)

    def unit_rows(p):
        inv = lax.rsqrt(jnp.sum(p * p, axis=-1, keepdims=True) + 1e-06)
        return p * inv, inv

    unit, _ = unit_rows(pool)
    r8 = iota((8, 1), 0)
    both = jnp.where(r8 < NT, pltpu.roll(unit[8:], 8 - NT, 0), unit[:8])
    emb[zx] = jnp.where(r8 < 2 * NT, both, 0.0).astype(BF)
    for p in zx_peers:
        send(emb.at[zx], emb.at[zx], 8, p)
    owner = s == y // 2
    mine = pf.at[lax.rem(y, 2)]

    @pl.when(owner)
    def _():
        for i, p in enumerate(sect_peers):
            send(mine, tbuf, 13 + i, p, rsem.at[9])
        c = pltpu.make_async_copy(mine, tbuf, lsem.at[0])
        c.start()
        c.wait()

    @pl.when(jnp.logical_not(owner))
    def _():
        await_bytes(tbuf, rsem.at[9])

    t_unit, t_inv = unit_rows(tbuf[...])
    t_emb = t_unit.astype(BF)
    m_ = mult[0]
    await_bytes(emb.at[pl.ds(0, NZX - 1)], rsem.at[8])
    ev = emb[...].reshape(NI, D)
    logits = m_ * dot_nt(t_emb, ev) + off[0]
    row = iota(logits.shape, 0)
    hit = posl == (NT * blk + row).astype(F32)
    label = jnp.where(hit, 1.0, -1.0)
    coef = -label * jax.nn.sigmoid(-label * logits)
    coef = jnp.where(row < NT, coef, 0.0).astype(BF)
    acc = dot_nn(coef, ev)
    arecv[s] = acc[:4]
    for p in sect_peers:
        send(arecv.at[s], arecv.at[s], 10, p)
    await_bytes(arecv.at[pl.ds(0, NS - 1)], rsem.at[10])
    g = m_ * jnp.sum(arecv[...], axis=0)
    u = t_unit[:4]
    gp = (g - u * jnp.sum(u * g, axis=-1, keepdims=True)) * t_inv[:4]
    dy = jnp.concatenate([gp, jnp.zeros_like(gp)], axis=0).astype(BF)
    for j in range(NY):
        dys[j, :, :NM] = dy[:, j * NM:(j + 1) * NM]
        dys[j, :, NM:] = dy[:, NY * NM:]
    dyr[y] = dys[y]
    for d in range(1, NY):
        send(dys.at[lax.rem(y + d, NY)], dyr.at[y], 11, y_peers[d - 1])
    wext = xpad[1, 0].astype(BF)
    await_bytes(dyr.at[pl.ds(0, NY - 1)], rsem.at[11])
    dv = dyr[...].reshape(NY * 8, NM + NE)
    take = (iota((NE, NZX), 0) == y * NZX + iota((NE, NZX), 1)).astype(F32).astype(BF)
    dext = dot_nn(dv[:, NM:], take).astype(BF)
    o = dot_nn(dv[:, :NM], wm[:, 1].reshape(NM, LP)) + dot_nn(dext, wext)
    for j in range(NY):
        osend[j] = o[8 * j:8 * j + 4]
    orecv[y] = osend[y]
    for d in range(1, NY):
        send(osend.at[lax.rem(y + d, NY)], orecv.at[y], 12, y_peers[d - 1])
    await_bytes(orecv.at[pl.ds(0, NY - 1)], rsem.at[12])
    out[...] = jnp.sum(orecv[...], axis=0)[:NT, :FFQ]

    await_bytes(hrecv.at[pl.ds(0, NS - 1)], ssem.at[0])
    await_bytes(wm.at[pl.ds(0, NZ - 1)], ssem.at[1])
    await_bytes(wx.at[pl.ds(0, NZ - 1)], ssem.at[2])
    await_bytes(wm.at[pl.ds(0, nx_in)], ssem.at[3])
    await_bytes(wx.at[pl.ds(0, nx_in)], ssem.at[4])
    await_bytes(hall.at[pl.ds(0, NY - 1)], ssem.at[5])
    await_bytes(precv.at[pl.ds(0, NS - 1)], ssem.at[6])
    await_bytes(full.at[pl.ds(0, NY - 1)], ssem.at[7])
    await_bytes(emb.at[pl.ds(0, NZX - 1)], ssem.at[8])

    @pl.when(owner)
    def _():
        for i in range(NS - 1):
            await_bytes(tbuf, ssem.at[13 + i])

    await_bytes(arecv.at[pl.ds(0, NS - 1)], ssem.at[10])
    await_bytes(dyr.at[pl.ds(0, NY - 1)], ssem.at[11])
    await_bytes(orecv.at[pl.ds(0, NY - 1)], ssem.at[12])


def on_device(hidden, w_txt, w_img, b_txt, b_img, mult, off, pos):
    NS, NZ, NX, NY = (lax.axis_size(a) for a in SECT_BLK)
    _, rows, FF = hidden.shape
    D = b_txt.shape[0]
    K = w_txt.shape[1]
    NZX = NZ * NX
    NM, NE = NZX * K8, NZX * NY
    FFQ = FF // NS
    LP = (FFQ + 3 + 127) // 128 * 128
    dims = (NS, NZ, NX, NY, FF)
    vm = pltpu.VMEM
    scratch = [
        vm((rows, FF), BF),
        vm((2, K, FF), BF),
        vm((K, LP), F32),
        vm((NZX, 2, K8, LP), BF),
        vm((NZX, 2, 1, LP), F32),
        vm((2, 1, NZX, LP), F32),
        vm((NS, 8, LP), BF),
        vm((NS, 8, LP), BF),
        vm((NY, 8, LP), BF),
        vm((NS, 16, NM + NE), F32),
        vm((NS, 16, NM + NE), F32),
        vm((NY, 16, NM + NE), F32),
        vm((2, 8, D), F32),
        vm((8, D), F32),
        vm((NZX, 8, D), BF),
        vm((NS, 4, D), F32),
        vm((NY, 8, NM + NE), BF),
        vm((NY, 8, NM + NE), BF),
        vm((NY, 4, LP), F32),
        vm((NY, 4, LP), F32),
        pltpu.SemaphoreType.DMA((3,)),
        pltpu.SemaphoreType.DMA((12 + NS,)),
        pltpu.SemaphoreType.DMA((13,)),
        pltpu.SemaphoreType.DMA((2 * (NZ - 1),)),
    ]
    any_ = pl.BlockSpec(memory_space=pl.ANY)
    vmem = pl.BlockSpec(memory_space=pltpu.VMEM)
    smem = pl.BlockSpec(memory_space=pltpu.SMEM)
    return pl.pallas_call(
        functools.partial(kernel, dims),
        out_shape=jax.ShapeDtypeStruct((NT, FFQ), F32),
        in_specs=[any_, any_, any_, vmem, vmem, smem, smem, vmem],
        out_specs=vmem,
        scratch_shapes=scratch,
        compiler_params=pltpu.CompilerParams(collective_id=0, has_side_effects=True),
    )(
        hidden[0], w_txt.T, w_img.T, b_txt[None], b_img[None], mult, off, pos[None]
    )


def solution(mesh):
    finer = Mesh(
        mesh.devices.reshape(mesh.shape["sect"], 4, 4, 8), ("sect", "blk_0", "blk_1", "blk_2")
    )
    placed = (P(SECT_BLK, None, None), P(None, BLK), P(None, BLK), P(), P(), P(), P(), P())
    return jax.shard_map(
        on_device, mesh=finer, in_specs=placed, out_specs=P(BLK, "sect"), check_vma=False
    )
```

```python
import functools

import jax
import jax.numpy as jnp
from jax import lax
from jax.experimental import pallas as pl
from jax.experimental.pallas import tpu as pltpu
from jax.sharding import Mesh
from jax.sharding import PartitionSpec as P

TXT_LEN = 64
NT = 3
K8 = 8
BF = jnp.bfloat16
F32 = jnp.float32
BLK = ("blk_0", "blk_1", "blk_2")
SECT_BLK = ("sect", "blk_0", "blk_1", "blk_2")
MESH = pl.DeviceIdType.MESH


def iota(shape, dim):
    return lax.broadcasted_iota(jnp.int32, shape, dim)


def dot_nn(a, b):
    return lax.dot_general(a, b, (((1,), (0,)), ((), ())), preferred_element_type=F32)


def dot_nt(a, b):
    return lax.dot_general(a, b, (((1,), (1,)), ((), ())), preferred_element_type=F32)


def unit_rows(p):
    inv = lax.rsqrt(jnp.sum(p * p, axis=-1, keepdims=True) + 1e-06)
    return p * inv, inv


def kernel(
    dims,
    hid, wt, wi, bt, bi, mult, off, pos,
    out,
    hv, wv, wtmp, wm, wx, xpad,
    hsend, hrecv, hall,
    pscr, psend, irecv, trecv, ifull, tfull,
    tbuf, emb, vsend, dyr, dls, osend, orecv,
    lsem, ssem, rsem, zsem,
):
    NS, NZ, NX, NY, FF = dims
    FFQ = FF // NS
    LP = wtmp.shape[1]
    NZX = NZ * NX
    NM = NZX * K8
    NE = NZX * NY
    s = lax.axis_index("sect")
    z = lax.axis_index("blk_0")
    x = lax.axis_index("blk_1")
    y = lax.axis_index("blk_2")
    zx = z * NX + x
    blk = zx * NY + y

    sect_peers = [{"sect": lax.rem(s + d, NS)} for d in range(1, NS)]
    y_far = sorted(range(1, NY), key=lambda d: -min(d, NY - d))
    y_peers = [{"blk_2": lax.rem(y + d, NY)} for d in y_far]
    z_peers = [{"blk_0": lax.rem(z + d, NZ)} for d in range(1, NZ)]
    x_peers = [{"blk_1": lax.rem(x + d, NX)} for d in range(1, NX)]
    zx_peers = []
    far = [(dz, dx) for dz in range(NZ) for dx in range(NX)][1:]
    far = sorted(far, key=lambda d: -2 * min(d[0], NZ - d[0]) - min(d[1], NX - d[1]))
    for dz, dx in far:
        zx_peers.append({"blk_0": lax.rem(z + dz, NZ), "blk_1": lax.rem(x + dx, NX)})

    loads = [
        pltpu.make_async_copy(wi, wv.at[0], lsem.at[0]),
        pltpu.make_async_copy(wt, wv.at[1], lsem.at[1]),
        pltpu.make_async_copy(hid, hv, lsem.at[2]),
    ]
    for c in loads:
        c.start()
    barrier = pltpu.get_barrier_semaphore()
    everyone = sect_peers + y_peers + x_peers + z_peers
    for p in everyone:
        pl.semaphore_signal(barrier, inc=1, device_id=p, device_id_type=MESH)

    def send(src, dst, k, peer, recv=None):
        pltpu.make_async_remote_copy(
            src_ref=src, dst_ref=dst, send_sem=ssem.at[k],
            recv_sem=rsem.at[k] if recv is None else recv,
            device_id=peer, device_id_type=MESH,
        ).start()

    def await_bytes(ref, sem):
        pltpu.make_async_copy(ref, ref, sem).wait()

    me = x * NZ + z
    for m, b in ((0, bi), (1, bt)):
        loads[m].wait()
        w32 = wv[m].astype(F32)
        wtmp[...] = jnp.zeros_like(wtmp)
        for q in range(NS):
            @pl.when(s == q)
            def _(q=q, w32=w32):
                wtmp[:, :FFQ] = w32[:, q * FFQ:(q + 1) * FFQ]
        v = wtmp[...]
        brow = jnp.broadcast_to(b[...][None], (K8 + 1, b.shape[0]))
        pick = iota(brow.shape, 1) == blk * (K8 + 1) + iota(brow.shape, 0)
        bcol = jnp.sum(jnp.where(pick, brow, 0.0), axis=1, keepdims=True)
        hi = bcol.astype(BF).astype(F32)
        lo = (bcol - hi).astype(BF).astype(F32)
        lane = iota(v.shape, 1)
        v = jnp.where(lane == FFQ, hi, v)
        v = jnp.where(lane == FFQ + 1, lo, v)
        v = jnp.where(lane == FFQ + 2, bcol - hi - lo, v)
        wm[me, m] = v[:K8].astype(BF)
        wx[me, m] = v[K8:].astype(BF).astype(F32)

    rows = hv.shape[0]
    r8 = iota((8, rows), 0)
    t8 = iota((8, rows), 1)
    is_txt = s == 0
    at = (lax.shift_right_logical(t8, 6) == r8).astype(F32)
    ai = (r8 == s - 1).astype(F32)
    f_txt = is_txt.astype(F32)
    a = (f_txt * at + (1.0 - f_txt) * ai).astype(BF)
    scale = jnp.where(is_txt, 1.0 / TXT_LEN, 1.0 / rows)
    loads[2].wait()
    hsum = dot_nn(a, hv[...]) * scale
    hsend[...] = jnp.zeros_like(hsend)
    for q in range(NS):
        hsend[q, :, :FFQ] = hsum[:4, q * FFQ:(q + 1) * FFQ].astype(BF)
    hrecv[s] = hsend[s]
    xpad[...] = jnp.zeros_like(xpad)
    dls[...] = jnp.zeros_like(dls)

    pl.semaphore_wait(barrier, len(everyone))

    for d in range(1, NS):
        send(hsend.at[lax.rem(s + d, NS)], hrecv.at[s], 0, sect_peers[d - 1])
    for i in range(NZ - 1):
        send(wm.at[me], wm.at[me], 1, z_peers[i], zsem.at[2 * i])
        send(wx.at[me], wx.at[me], 2, z_peers[i], zsem.at[2 * i + 1])
    for i in range(NX - 1):
        send(wm.at[me], wm.at[me], 3, x_peers[i])
        send(wx.at[me], wx.at[me], 4, x_peers[i])
    await_bytes(hrecv.at[pl.ds(0, NS - 1)], rsem.at[0])
    hr = hrecv[...].astype(F32)
    hq = jnp.concatenate([hr[0], hr[1] + hr[2] + hr[3]], axis=0)
    lane = iota(hq.shape, 1)
    ones = ((lane >= FFQ) & (lane < FFQ + 3)).astype(F32) * f_txt
    hall[y] = (hq + ones).astype(BF)
    for p in y_peers:
        send(hall.at[y], hall.at[y], 5, p)
    for i in range(NZ - 1):
        zz = lax.rem(z + NZ - (i + 1), NZ)
        sl = x * NZ + zz
        await_bytes(wm.at[sl], zsem.at[2 * i])
        await_bytes(wx.at[sl], zsem.at[2 * i + 1])
        for p in x_peers:
            send(wm.at[sl], wm.at[sl], 3, p)
            send(wx.at[sl], wx.at[sl], 4, p)
    await_bytes(hall.at[pl.ds(0, NY - 1)], rsem.at[5])
    hrows = hall[...].reshape(NY * 8, LP)
    nx_in = (NX - 1) * NZ
    await_bytes(wm.at[pl.ds(0, nx_in)], rsem.at[3])
    await_bytes(wx.at[pl.ds(0, nx_in)], rsem.at[4])

    parts = []
    for m in range(2):
        for j in range(NZX):
            wtmp[0:1, :] = wx[j, m]
            xpad[m, j:j + 1, :] = wtmp[0:1, :]
    for m in range(2):
        pm = dot_nt(hrows, wm[:, m].reshape(NM, LP))
        pe = dot_nt(hrows, xpad[m].astype(BF))
        parts.append((pm, pe))
    r64 = lax.bitwise_and(iota((NY * 8, 1), 0), 7)
    pe = jnp.where(r64 < 4, parts[1][1], parts[0][1])
    place = (iota((NZX, NE), 1) == y * NZX + iota((NZX, NE), 0)).astype(F32)
    pscr[:NY * 8] = jnp.where(r64 < 4, parts[1][0], parts[0][0])
    pscr[NY * 8:] = lax.dot_general(
        pe, place, (((1,), (0,)), ((), ())), preferred_element_type=F32,
        precision=lax.Precision.HIGHEST,
    )
    for r in range(NT):
        for to, row in ((r, r), (NT + r, 4 + r)):
            psend[to, :, :NM] = pscr[pl.ds(row, NY, stride=8), :]
            psend[to, :, NM:] = pscr[pl.ds(NY * 8 + row, NY, stride=8), :]

    for d in range(1, NS):
        sp = lax.rem(s + d, NS)

        @pl.when(sp != 0)
        def _(d=d, sp=sp):
            send(psend.at[NT - 1 + sp], irecv.at[s], 6, sect_peers[d - 1])

        @pl.when(sp == 0)
        def _(d=d):
            send(psend.at[pl.ds(0, NT)], trecv.at[s], 7, sect_peers[d - 1])

    m_ = mult[0]
    n_dy = NY * (NS - 1)

    @pl.when(is_txt)
    def _():
        tbuf[...] = jnp.zeros_like(tbuf)
        trecv[0] = psend[:NT]
        await_bytes(trecv.at[pl.ds(0, NS - 1)], rsem.at[7])
        tfull[y] = jnp.sum(trecv[...], axis=0)
        for p in y_peers:
            send(tfull.at[y], tfull.at[y], 8, p)
        own = iota((NY, NM + NE), 0) == y
        await_bytes(tfull.at[pl.ds(0, NY - 1)], rsem.at[8])
        for r in range(NT):
            extra = jnp.zeros((1, NE), F32)
            for j in range(NY):
                v = jnp.sum(jnp.where(own, tfull[j, r], 0.0), axis=0, keepdims=True)
                tbuf[r:r + 1, j * NM:(j + 1) * NM] = v[:, :NM]
                extra = extra + v[:, NM:]
            tbuf[r:r + 1, NY * NM:] = extra
        for i, p in enumerate(sect_peers):
            send(tbuf, tbuf, 13 + i, p, rsem.at[9])
        await_bytes(dyr, rsem.at[11])
        await_bytes(irecv.at[pl.ds(0, NS - 1)], ssem.at[6])
        await_bytes(tfull.at[pl.ds(0, NY - 1)], ssem.at[8])
        for i in range(NS - 1):
            await_bytes(tbuf, ssem.at[13 + i])

    @pl.when(jnp.logical_not(is_txt))
    def _():
        irecv[s] = psend[NT - 1 + s]
        await_bytes(irecv.at[pl.ds(0, NS - 1)], rsem.at[6])
        ifull[y] = jnp.sum(irecv[...], axis=0)
        for p in y_peers:
            send(ifull.at[y], ifull.at[y], 8, p)
        await_bytes(ifull.at[pl.ds(0, NY - 1)], rsem.at[8])
        fv = ifull[...]
        extra = jnp.sum(fv[:, :, NM:], axis=0)
        unit, _ = unit_rows(jnp.concatenate([fv[j, :, :NM] for j in range(NY)] + [extra], axis=1))
        emb[zx] = unit.astype(BF)
        for p in zx_peers:
            send(emb.at[zx], emb.at[zx], 10, p)
        NI = NZX * 8
        at_img = pos[0:NI]
        for j in range(1, NS - 1):
            at_img = jnp.where(s == j + 1, pos[j * NI:(j + 1) * NI], at_img)
        hit = at_img[None] == NT * blk + iota((4, NI), 0)
        label = jnp.where(hit, 1.0, -1.0)
        await_bytes(tbuf, rsem.at[9])
        t_unit, t_inv = unit_rows(tbuf[...])
        t_emb = t_unit.astype(BF)
        await_bytes(emb.at[pl.ds(0, NZX - 1)], rsem.at[10])
        ev = emb[...].reshape(NI, NY * NM + NE)
        logits = m_ * dot_nt(t_emb, ev) + off[0]
        coef = -label * jax.nn.sigmoid(-label * logits)
        coef = jnp.where(iota(coef.shape, 0) < NT, coef, 0.0).astype(BF)
        g = m_ * dot_nn(coef, ev)
        gp = (g - t_unit * jnp.sum(t_unit * g, axis=-1, keepdims=True)) * t_inv
        for j in range(NY):
            vsend[j, :, :NM] = gp[:, j * NM:(j + 1) * NM]
            vsend[j, :, NM:] = gp[:, NY * NM:]
        slot = y * (NS - 1) + s - 1
        dyr[slot] = vsend[y]
        for dd in y_far + [0]:
            yp = lax.rem(y + dd, NY)
            for ds in range(NS):
                if dd or ds:
                    peer = {"sect": lax.rem(s + ds, NS), "blk_2": yp}
                    send(vsend.at[yp], dyr.at[slot], 13 + ds, peer, rsem.at[11])
        await_bytes(dyr.at[pl.ds(0, n_dy - 1)], rsem.at[11])
        await_bytes(ifull.at[pl.ds(0, NY - 1)], ssem.at[8])
        await_bytes(emb.at[pl.ds(0, NZX - 1)], ssem.at[10])
        await_bytes(vsend.at[pl.ds(0, NY - 1)], ssem.at[13])
        for ds in range(1, NS):
            await_bytes(vsend, ssem.at[13 + ds])
        await_bytes(irecv.at[pl.ds(0, NS - 2)], ssem.at[6])
        await_bytes(psend.at[pl.ds(0, NT)], ssem.at[7])

    for j in range(NY):
        v = dyr[3 * j] + dyr[3 * j + 1] + dyr[3 * j + 2]
        dls[8 * j:8 * j + 4, :] = v
    dv = dls[...].astype(BF)
    take = (iota((NE, NZX), 0) == y * NZX + iota((NE, NZX), 1)).astype(F32).astype(BF)
    dext = dot_nn(dv[:, NM:], take).astype(BF)
    o = dot_nn(dv[:, :NM], wm[:, 1].reshape(NM, LP)) + dot_nn(dext, xpad[1].astype(BF))
    for j in range(NY):
        osend[j] = o[8 * j:8 * j + 4].astype(BF)
    orecv[y] = osend[y]
    for d, p in zip(y_far, y_peers):
        send(osend.at[lax.rem(y + d, NY)], orecv.at[y], 12, p)
    await_bytes(orecv.at[pl.ds(0, NY - 1)], rsem.at[12])
    out[...] = jnp.sum(orecv[...].astype(F32), axis=0)[:NT, :FFQ]

    await_bytes(hrecv.at[pl.ds(0, NS - 1)], ssem.at[0])
    await_bytes(wm.at[pl.ds(0, NZ - 1)], ssem.at[1])
    await_bytes(wx.at[pl.ds(0, NZ - 1)], ssem.at[2])
    await_bytes(wm.at[pl.ds(0, nx_in)], ssem.at[3])
    await_bytes(wx.at[pl.ds(0, nx_in)], ssem.at[4])
    await_bytes(hall.at[pl.ds(0, NY - 1)], ssem.at[5])
    await_bytes(orecv.at[pl.ds(0, NY - 1)], ssem.at[12])


def on_device(hidden, w_txt, w_img, b_txt, b_img, mult, off, pos):
    NS, NZ, NX, NY = (lax.axis_size(a) for a in SECT_BLK)
    _, rows, FF = hidden.shape
    D = b_txt.shape[0]
    K = w_txt.shape[1]
    NZX = NZ * NX
    NM, NE = NZX * K8, NZX * NY
    FFQ = FF // NS
    LP = (FFQ + 3 + 127) // 128 * 128
    dims = (NS, NZ, NX, NY, FF)
    vm = pltpu.VMEM
    scratch = [
        vm((rows, FF), BF),
        vm((2, K, FF), BF),
        vm((K, LP), F32),
        vm((NZX, 2, K8, LP), BF),
        vm((NZX, 2, 1, LP), F32),
        vm((2, NZX, LP), F32),
        vm((NS, 4, LP), BF),
        vm((NS, 4, LP), BF),
        vm((NY, 8, LP), BF),
        vm((2 * NY * 8, NM), F32),
        vm((2 * NT, NY, NM + NE), F32),
        vm((NS, NY, NM + NE), F32),
        vm((NS, NT, NY, NM + NE), F32),
        vm((NY, NY, NM + NE), F32),
        vm((NY, NT, NY, NM + NE), F32),
        vm((4, D), F32),
        vm((NZX, 8, D), BF),
        vm((NY, 4, NM + NE), F32),
        vm((NY * (NS - 1), 4, NM + NE), F32),
        vm((NY * 8, NM + NE), F32),
        vm((NY, 4, LP), BF),
        vm((NY, 4, LP), BF),
        pltpu.SemaphoreType.DMA((3,)),
        pltpu.SemaphoreType.DMA((13 + NS,)),
        pltpu.SemaphoreType.DMA((13,)),
        pltpu.SemaphoreType.DMA((2 * (NZ - 1),)),
    ]
    any_ = pl.BlockSpec(memory_space=pl.ANY)
    vmem = pl.BlockSpec(memory_space=pltpu.VMEM)
    smem = pl.BlockSpec(memory_space=pltpu.SMEM)
    return pl.pallas_call(
        functools.partial(kernel, dims),
        out_shape=jax.ShapeDtypeStruct((NT, FFQ), F32),
        in_specs=[any_, any_, any_, vmem, vmem, smem, smem, vmem],
        out_specs=vmem,
        scratch_shapes=scratch,
        compiler_params=pltpu.CompilerParams(collective_id=0, has_side_effects=True),
    )(
        hidden[0], w_txt.T, w_img.T, b_txt, b_img, mult, off, pos
    )


def solution(mesh):
    finer = Mesh(
        mesh.devices.reshape(mesh.shape["sect"], 4, 4, 8), ("sect", "blk_0", "blk_1", "blk_2")
    )
    placed = (P(SECT_BLK, None, None), P(None, BLK), P(None, BLK), P(), P(), P(), P(), P())
    return jax.shard_map(
        on_device, mesh=finer, in_specs=placed, out_specs=P(BLK, "sect"), check_vma=False
    )
```

```python
import functools

import jax
import jax.numpy as jnp
from jax import lax
from jax.experimental import pallas as pl
from jax.experimental.pallas import tpu as pltpu
from jax.sharding import Mesh
from jax.sharding import PartitionSpec as P

TXT_LEN = 64
NT = 3
K8 = 8
BF = jnp.bfloat16
F32 = jnp.float32
BLK = ("blk_0", "blk_1", "blk_2")
SECT_BLK = ("sect", "blk_0", "blk_1", "blk_2")
MESH = pl.DeviceIdType.MESH
DY = F32
OT = F32


def iota(shape, dim):
    return lax.broadcasted_iota(jnp.int32, shape, dim)


def dot_nn(a, b):
    return lax.dot_general(a, b, (((1,), (0,)), ((), ())), preferred_element_type=F32)


def dot_nt(a, b):
    return lax.dot_general(a, b, (((1,), (1,)), ((), ())), preferred_element_type=F32)


def unit_rows(p):
    inv = lax.rsqrt(jnp.sum(p * p, axis=-1, keepdims=True) + 1e-06)
    return p * inv, inv


def kernel(
    dims,
    hid, wt, wi, bt, bi, mult, off, pos,
    out,
    hv, wv, wtmp, wm, wx, xpad,
    hsend, hrecv, hall,
    pscr, psend, irecv, trecv, ifull, tfull,
    tbuf, emb, emit, dyr, dls, osend, orecv,
    wf, we, wes, tm, te,
    lsem, ssem, rsem, zsem, xsem, ysem,
):
    NS, NZ, NX, NY, FF = dims
    FFQ = FF // NS
    LP = wtmp.shape[1]
    NZX = NZ * NX
    NM = NZX * K8
    NE = NZX * NY
    s = lax.axis_index("sect")
    z = lax.axis_index("blk_0")
    x = lax.axis_index("blk_1")
    y = lax.axis_index("blk_2")
    zx = z * NX + x
    blk = zx * NY + y

    sect_peers = [{"sect": lax.rem(s + d, NS)} for d in range(1, NS)]
    y_far = sorted(range(1, NY), key=lambda d: -min(d, NY - d))
    y_peers = [{"blk_2": lax.rem(y + d, NY)} for d in y_far]
    z_peers = [{"blk_0": lax.rem(z + d, NZ)} for d in range(1, NZ)]
    x_far = sorted(range(1, NX), key=lambda d: -min(d, NX - d))
    x_peers = [{"blk_1": lax.rem(x + d, NX)} for d in x_far]
    zx_peers = []
    far = [(dz, dx) for dz in range(NZ) for dx in range(NX)][1:]
    far = sorted(far, key=lambda d: -2 * min(d[0], NZ - d[0]) - min(d[1], NX - d[1]))
    for dz, dx in far:
        zx_peers.append({"blk_0": lax.rem(z + dz, NZ), "blk_1": lax.rem(x + dx, NX)})

    loads = [
        pltpu.make_async_copy(wi, wv.at[0], lsem.at[0]),
        pltpu.make_async_copy(wt, wv.at[1], lsem.at[1]),
        pltpu.make_async_copy(hid, hv, lsem.at[2]),
    ]
    for c in loads:
        c.start()
    barrier = pltpu.get_barrier_semaphore()
    everyone = sect_peers + y_peers + x_peers + z_peers
    for p in everyone:
        pl.semaphore_signal(barrier, inc=1, device_id=p, device_id_type=MESH)

    def send(src, dst, k, peer, recv=None):
        pltpu.make_async_remote_copy(
            src_ref=src, dst_ref=dst, send_sem=ssem.at[k],
            recv_sem=rsem.at[k] if recv is None else recv,
            device_id=peer, device_id_type=MESH,
        ).start()

    def await_bytes(ref, sem):
        pltpu.make_async_copy(ref, ref, sem).wait()

    me = x * NZ + z
    for m, b in ((0, bi), (1, bt)):
        loads[m].wait()
        w32 = wv[m].astype(F32)
        wtmp[...] = jnp.zeros_like(wtmp)
        for q in range(NS):
            @pl.when(s == q)
            def _(q=q, w32=w32):
                wtmp[:, :FFQ] = w32[:, q * FFQ:(q + 1) * FFQ]
        v = wtmp[...]
        brow = jnp.broadcast_to(b[...][None], (K8 + 1, b.shape[0]))
        pick = iota(brow.shape, 1) == blk * (K8 + 1) + iota(brow.shape, 0)
        bcol = jnp.sum(jnp.where(pick, brow, 0.0), axis=1, keepdims=True)
        hi = bcol.astype(BF).astype(F32)
        lo = (bcol - hi).astype(BF).astype(F32)
        lane = iota(v.shape, 1)
        v = jnp.where(lane == FFQ, hi, v)
        v = jnp.where(lane == FFQ + 1, lo, v)
        v = jnp.where(lane == FFQ + 2, bcol - hi - lo, v)
        wm[m, me] = v[:K8].astype(BF)
        wx[m, me] = v[K8:].astype(BF).astype(F32)

    rows = hv.shape[0]
    r8 = iota((8, rows), 0)
    t8 = iota((8, rows), 1)
    is_txt = s == 0
    at = (lax.shift_right_logical(t8, 6) == r8).astype(F32)
    ai = (r8 == s - 1).astype(F32)
    f_txt = is_txt.astype(F32)
    a = (f_txt * at + (1.0 - f_txt) * ai).astype(BF)
    scale = jnp.where(is_txt, 1.0 / TXT_LEN, 1.0 / rows)
    loads[2].wait()
    hsum = dot_nn(a, hv[...]) * scale
    hsend[...] = jnp.zeros_like(hsend)
    for q in range(NS):
        hsend[q, :, :FFQ] = hsum[:4, q * FFQ:(q + 1) * FFQ].astype(BF)
    hrecv[s] = hsend[s]
    n_m, n_e = NY * NZ * K8, NY * NZ
    c_m, c_e = iota((NY * NM, n_m), 1), iota((NE, n_e), 1)
    per_y, per_z = NZ * K8, NZ
    t_m = iota((NY * NM, n_m), 0) == c_m // per_y * NM + x * per_y + lax.rem(c_m, per_y)
    t_e = iota((NE, n_e), 0) == c_e // per_z * NZX + x * per_z + lax.rem(c_e, per_z)
    tm[...] = t_m.astype(F32).astype(BF)
    te[...] = t_e.astype(F32).astype(BF)
    xpad[...] = jnp.zeros_like(xpad)
    dls[...] = jnp.zeros_like(dls)

    pl.semaphore_wait(barrier, len(everyone))

    for d in range(1, NS):
        send(hsend.at[lax.rem(s + d, NS)], hrecv.at[s], 0, sect_peers[d - 1])
    for m in range(2):
        for i in range(NZ - 1):
            send(wm.at[m, me], wm.at[m, me], 1, z_peers[i], zsem.at[m, i, 0])
            send(wx.at[m, me], wx.at[m, me], 2, z_peers[i], zsem.at[m, i, 1])
        for p in x_peers:
            send(wm.at[m, me], wm.at[m, me], 3 + 16 * m, p, xsem.at[m, 0])
            send(wx.at[m, me], wx.at[m, me], 4 + 16 * m, p, xsem.at[m, 1])
    await_bytes(hrecv.at[pl.ds(0, NS - 1)], rsem.at[0])
    hr = hrecv[...].astype(F32)
    hq = jnp.concatenate([hr[0], hr[1] + hr[2] + hr[3]], axis=0)
    lane = iota(hq.shape, 1)
    ones = ((lane >= FFQ) & (lane < FFQ + 3)).astype(F32) * f_txt
    hall[y] = (hq + ones).astype(BF)
    for p in y_peers:
        send(hall.at[y], hall.at[y], 5, p)
    for m in range(2):
        for i in range(NZ - 1):
            sl = x * NZ + lax.rem(z + NZ - (i + 1), NZ)
            await_bytes(wm.at[m, sl], zsem.at[m, i, 0])
            await_bytes(wx.at[m, sl], zsem.at[m, i, 1])
            for p in x_peers:
                send(wm.at[m, sl], wm.at[m, sl], 3 + 16 * m, p, xsem.at[m, 0])
                send(wx.at[m, sl], wx.at[m, sl], 4 + 16 * m, p, xsem.at[m, 1])
    await_bytes(hall.at[pl.ds(0, NY - 1)], rsem.at[5])
    hrows = hall[...].reshape(NY * 8, LP)
    nx_in = (NX - 1) * NZ

    wf[y] = wm[1, pl.ds(x * NZ, NZ)].reshape(NZ * K8, LP)
    for j in range(NZ):
        we[y, j:j + 1, :] = wx[1, x * NZ + j]

    def ring_send(t):
        for k, far, hop in ((0, NY // 2, 1), (1, NY - 1 - NY // 2, NY - 1)):
            if t <= far:
                c = lax.rem(y + (NY - hop) * (t - 1), NY)
                p = {"blk_2": lax.rem(y + hop, NY)}
                send(wf.at[c], wf.at[c], 10 + k, p, ysem.at[k, t - 1, 0])
                send(we.at[c], we.at[c], 14 + k, p, ysem.at[k, t - 1, 1])

    def ring_wait(t):
        for k, far, hop in ((0, NY // 2, 1), (1, NY - 1 - NY // 2, NY - 1)):
            if t <= far:
                c = lax.rem(y + (NY - hop) * t, NY)
                await_bytes(wf.at[c], ysem.at[k, t - 1, 0])
                await_bytes(we.at[c], ysem.at[k, t - 1, 1])

    ring_send(1)

    place = (iota((NZX, NE), 1) == y * NZX + iota((NZX, NE), 0)).astype(F32)

    def tile(m, r0):
        await_bytes(wm.at[m, pl.ds(0, nx_in)], xsem.at[m, 0])
        await_bytes(wx.at[m, pl.ds(0, nx_in)], xsem.at[m, 1])
        for j in range(NZX):
            xpad[m, j:j + 1, :] = wx[m, j]
        pe = dot_nt(hrows, xpad[m].astype(BF))
        pscr[m, :NY * 8] = dot_nt(hrows, wm[m].reshape(NM, LP))
        pscr[m, NY * 8:] = lax.dot_general(
            pe, place, (((1,), (0,)), ((), ())), preferred_element_type=F32,
            precision=lax.Precision.HIGHEST,
        )
        for r in range(NT):
            to = r if m else NT + r
            psend[to, :, :NM] = pscr[m, pl.ds(r0 + r, NY, stride=8), :]
            psend[to, :, NM:] = pscr[m, pl.ds(NY * 8 + r0 + r, NY, stride=8), :]

    tile(0, 4)
    for d in range(1, NS):
        sp = lax.rem(s + d, NS)

        @pl.when(sp != 0)
        def _(d=d, sp=sp):
            send(psend.at[NT - 1 + sp], irecv.at[s], 6, sect_peers[d - 1])
    tile(1, 0)
    for d in range(1, NS):
        sp = lax.rem(s + d, NS)

        @pl.when(sp == 0)
        def _(d=d):
            send(psend.at[pl.ds(0, NT)], trecv.at[s], 7, sect_peers[d - 1])

    m_ = mult[0]
    n_dy = NX * (NS - 1)

    @pl.when(is_txt)
    def _():
        tbuf[...] = jnp.zeros_like(tbuf)
        trecv[0] = psend[:NT]
        await_bytes(trecv.at[pl.ds(0, NS - 1)], rsem.at[7])
        tfull[y] = jnp.sum(trecv[...], axis=0)
        for p in y_peers:
            send(tfull.at[y], tfull.at[y], 8, p)
        ring_wait(1)
        ring_send(2)
        own = iota((NY, NM + NE), 0) == y
        await_bytes(tfull.at[pl.ds(0, NY - 1)], rsem.at[8])
        for r in range(NT):
            extra = jnp.zeros((1, NE), F32)
            for j in range(NY):
                v = jnp.sum(jnp.where(own, tfull[j, r], 0.0), axis=0, keepdims=True)
                tbuf[r:r + 1, j * NM:(j + 1) * NM] = v[:, :NM]
                extra = extra + v[:, NM:]
            tbuf[r:r + 1, NY * NM:] = extra
        for i, p in enumerate(sect_peers):
            send(tbuf, tbuf, 16 + i, p, rsem.at[9])
        ring_wait(2)
        ring_send(3)
        ring_wait(3)
        ring_send(4)
        await_bytes(dyr, rsem.at[11])
        await_bytes(irecv.at[pl.ds(0, NS - 1)], ssem.at[6])
        await_bytes(tfull.at[pl.ds(0, NY - 1)], ssem.at[8])
        for i in range(NS - 1):
            await_bytes(tbuf, ssem.at[16 + i])

    @pl.when(jnp.logical_not(is_txt))
    def _():
        irecv[s] = psend[NT - 1 + s]
        await_bytes(irecv.at[pl.ds(0, NS - 1)], rsem.at[6])
        ifull[y] = jnp.sum(irecv[...], axis=0)
        for p in y_peers:
            send(ifull.at[y], ifull.at[y], 8, p)
        ring_wait(1)
        ring_send(2)
        await_bytes(ifull.at[pl.ds(0, NY - 1)], rsem.at[8])
        fv = ifull[...]
        extra = jnp.sum(fv[:, :, NM:], axis=0)
        unit, _ = unit_rows(jnp.concatenate([fv[j, :, :NM] for j in range(NY)] + [extra], axis=1))
        emb[zx] = unit.astype(BF)
        for p in zx_peers:
            send(emb.at[zx], emb.at[zx], 9, p, rsem.at[10])
        ring_wait(2)
        ring_send(3)
        NI = NZX * 8
        at_img = pos[0:NI]
        for j in range(1, NS - 1):
            at_img = jnp.where(s == j + 1, pos[j * NI:(j + 1) * NI], at_img)
        hit = at_img[None] == NT * blk + iota((4, NI), 0)
        label = jnp.where(hit, 1.0, -1.0)
        await_bytes(tbuf, rsem.at[9])
        t_unit, t_inv = unit_rows(tbuf[...])
        t_emb = t_unit.astype(BF)
        ring_wait(3)
        ring_send(4)
        await_bytes(emb.at[pl.ds(0, NZX - 1)], rsem.at[10])
        ev = emb[...].reshape(NI, NY * NM + NE)
        logits = m_ * dot_nt(t_emb, ev) + off[0]
        coef = -label * jax.nn.sigmoid(-label * logits)
        coef = jnp.where(iota(coef.shape, 0) < NT, coef, 0.0).astype(BF)
        g = m_ * dot_nn(coef, ev)
        gp = (g - t_unit * jnp.sum(t_unit * g, axis=-1, keepdims=True)) * t_inv
        slot = x * (NS - 1) + s - 1
        dyr[slot] = gp.astype(DY)
        for dx in x_far + [0]:
            for ds in range(NS):
                if dx or ds:
                    peer = {"sect": lax.rem(s + ds, NS), "blk_1": lax.rem(x + dx, NX)}
                    send(dyr.at[slot], dyr.at[slot], 13, peer, rsem.at[11])
        await_bytes(dyr.at[pl.ds(0, n_dy - 1)], rsem.at[11])
        await_bytes(ifull.at[pl.ds(0, NY - 1)], ssem.at[8])
        await_bytes(emb.at[pl.ds(0, NZX - 1)], ssem.at[9])
        await_bytes(emit.at[pl.ds(0, NX * NS - 1)], ssem.at[13])
        await_bytes(irecv.at[pl.ds(0, NS - 2)], ssem.at[6])
        await_bytes(psend.at[pl.ds(0, NT)], ssem.at[7])

    for j in range(NX):
        v = sum(dyr[(NS - 1) * j + i].astype(F32) for i in range(NS - 1))
        dls[4 * j:4 * j + 4, :] = v
    dv = dls[...].astype(BF)
    d_m = dot_nn(dv[:, :NY * NM], tm[...]).astype(BF)
    d_e = dot_nn(dv[:, NY * NM:], te[...]).astype(BF)
    ring_wait(4)
    for j in range(NY):
        wes[NZ * j:NZ * (j + 1), :] = we[j]
    o = dot_nn(d_m, wf[...].reshape(n_m, LP)) + dot_nn(d_e, wes[...].astype(BF))
    for j in range(NX):
        osend[j] = o[4 * j:4 * j + 4].astype(OT)
    orecv[x] = osend[x]
    for d, p in zip(x_far, x_peers):
        send(osend.at[lax.rem(x + d, NX)], orecv.at[x], 12, p)
    await_bytes(orecv.at[pl.ds(0, NX - 1)], rsem.at[12])
    out[...] = jnp.sum(orecv[...].astype(F32), axis=0)[:NT, :FFQ]

    await_bytes(hrecv.at[pl.ds(0, NS - 1)], ssem.at[0])
    for k, ref in ((1, wm), (2, wx)):
        n_z = 2 * (NZ - 1)
        await_bytes(ref.at[0, pl.ds(0, n_z)], ssem.at[k])
    for k, ref in ((3, wm), (4, wx), (19, wm), (20, wx)):
        await_bytes(ref.at[0, pl.ds(0, nx_in)], ssem.at[k])
    for k, far in ((0, NY // 2), (1, NY - 1 - NY // 2)):
        await_bytes(wf.at[pl.ds(0, far)], ssem.at[10 + k])
        await_bytes(we.at[pl.ds(0, far)], ssem.at[14 + k])
    await_bytes(hall.at[pl.ds(0, NY - 1)], ssem.at[5])
    await_bytes(orecv.at[pl.ds(0, NX - 1)], ssem.at[12])


def on_device(hidden, w_txt, w_img, b_txt, b_img, mult, off, pos):
    NS, NZ, NX, NY = (lax.axis_size(a) for a in SECT_BLK)
    _, rows, FF = hidden.shape
    D = b_txt.shape[0]
    K = w_txt.shape[1]
    NZX = NZ * NX
    NM, NE = NZX * K8, NZX * NY
    FFQ = FF // NS
    LP = (FFQ + 3 + 127) // 128 * 128
    dims = (NS, NZ, NX, NY, FF)
    vm = pltpu.VMEM
    scratch = [
        vm((rows, FF), BF),
        vm((2, K, FF), BF),
        vm((K, LP), F32),
        vm((2, NZX, K8, LP), BF),
        vm((2, NZX, 1, LP), F32),
        vm((2, NZX, LP), F32),
        vm((NS, 4, LP), BF),
        vm((NS, 4, LP), BF),
        vm((NY, 8, LP), BF),
        vm((2, 2 * NY * 8, NM), F32),
        vm((2 * NT, NY, NM + NE), F32),
        vm((NS, NY, NM + NE), F32),
        vm((NS, NT, NY, NM + NE), F32),
        vm((NY, NY, NM + NE), F32),
        vm((NY, NT, NY, NM + NE), F32),
        vm((4, D), F32),
        vm((NZX, 8, D), BF),
        vm((NX * NS, 4, D), DY),
        vm((NX * (NS - 1), 4, D), DY),
        vm((NX * 4, D), F32),
        vm((NX, 4, LP), OT),
        vm((NX, 4, LP), OT),
        vm((NY, NZ * K8, LP), BF),
        vm((NY, NZ, LP), F32),
        vm((NY * NZ, LP), F32),
        vm((NY * NM, NY * NZ * K8), BF),
        vm((NE, NY * NZ), BF),
        pltpu.SemaphoreType.DMA((3,)),
        pltpu.SemaphoreType.DMA((21,)),
        pltpu.SemaphoreType.DMA((13,)),
        pltpu.SemaphoreType.DMA((2, NZ - 1, 2)),
        pltpu.SemaphoreType.DMA((2, 2)),
        pltpu.SemaphoreType.DMA((2, NY // 2, 2)),
    ]
    any_ = pl.BlockSpec(memory_space=pl.ANY)
    vmem = pl.BlockSpec(memory_space=pltpu.VMEM)
    smem = pl.BlockSpec(memory_space=pltpu.SMEM)
    return pl.pallas_call(
        functools.partial(kernel, dims),
        out_shape=jax.ShapeDtypeStruct((NT, FFQ), F32),
        in_specs=[any_, any_, any_, vmem, vmem, smem, smem, vmem],
        out_specs=vmem,
        scratch_shapes=scratch,
        compiler_params=pltpu.CompilerParams(collective_id=0, has_side_effects=True),
    )(
        hidden[0], w_txt.T, w_img.T, b_txt, b_img, mult, off, pos
    )


def solution(mesh):
    finer = Mesh(
        mesh.devices.reshape(mesh.shape["sect"], 4, 4, 8), ("sect", "blk_0", "blk_1", "blk_2")
    )
    placed = (P(SECT_BLK, None, None), P(None, BLK), P(None, BLK), P(), P(), P(), P(), P())
    return jax.shard_map(
        on_device, mesh=finer, in_specs=placed, out_specs=P(BLK, "sect"), check_vma=False
    )
```

```python
import functools

import jax
import jax.numpy as jnp
from jax import lax
from jax.experimental import pallas as pl
from jax.experimental.pallas import tpu as pltpu
from jax.sharding import Mesh
from jax.sharding import PartitionSpec as P

TXT_LEN = 64
NT = 3
K8 = 8
BF = jnp.bfloat16
F32 = jnp.float32
BLK = ("blk_0", "blk_1", "blk_2")
SECT_BLK = ("sect", "blk_0", "blk_1", "blk_2")
MESH = pl.DeviceIdType.MESH
DY = F32
OT = F32


def iota(shape, dim):
    return lax.broadcasted_iota(jnp.int32, shape, dim)


def dot_nn(a, b):
    return lax.dot_general(a, b, (((1,), (0,)), ((), ())), preferred_element_type=F32)


def dot_nt(a, b):
    return lax.dot_general(a, b, (((1,), (1,)), ((), ())), preferred_element_type=F32)


def unit_rows(p):
    inv = lax.rsqrt(jnp.sum(p * p, axis=-1, keepdims=True) + 1e-06)
    return p * inv, inv


def kernel(
    dims,
    hid, wt, wi, bt, bi, mult, off, pos,
    out,
    hv, wv, wtmp, wm, wx, xpad,
    hsend, hrecv, hall,
    xe, pscr, psend, ptx, irecv, trecv, ifull, tsum, tfull,
    tbuf, emb, emit, dyr, dls, osend, orecv,
    wf, we, wes, tm, te,
    lsem, ssem, rsem, zsem, xsem, ysem,
):
    NS, NZ, NX, NY, FF = dims
    FFQ = FF // NS
    LP = wtmp.shape[1]
    NZX = NZ * NX
    NM = NZX * K8
    NE = NZX * NY
    s = lax.axis_index("sect")
    z = lax.axis_index("blk_0")
    x = lax.axis_index("blk_1")
    y = lax.axis_index("blk_2")
    zx = z * NX + x
    blk = zx * NY + y

    sect_peers = [{"sect": lax.rem(s + d, NS)} for d in range(1, NS)]
    y_far = sorted(range(1, NY), key=lambda d: -min(d, NY - d))
    y_peers = [{"blk_2": lax.rem(y + d, NY)} for d in y_far]
    z_peers = [{"blk_0": lax.rem(z + d, NZ)} for d in range(1, NZ)]
    x_far = sorted(range(1, NX), key=lambda d: -min(d, NX - d))
    x_peers = [{"blk_1": lax.rem(x + d, NX)} for d in x_far]
    zx_peers = []
    far = [(dz, dx) for dz in range(NZ) for dx in range(NX)][1:]
    far = sorted(far, key=lambda d: -2 * min(d[0], NZ - d[0]) - min(d[1], NX - d[1]))
    for dz, dx in far:
        zx_peers.append({"blk_0": lax.rem(z + dz, NZ), "blk_1": lax.rem(x + dx, NX)})

    loads = [
        pltpu.make_async_copy(wi, wv.at[0], lsem.at[0]),
        pltpu.make_async_copy(wt, wv.at[1], lsem.at[1]),
        pltpu.make_async_copy(hid, hv, lsem.at[2]),
    ]
    for c in loads:
        c.start()
    barrier = pltpu.get_barrier_semaphore()
    everyone = sect_peers + y_peers + x_peers + z_peers
    for p in everyone:
        pl.semaphore_signal(barrier, inc=1, device_id=p, device_id_type=MESH)

    def send(src, dst, k, peer, recv=None):
        pltpu.make_async_remote_copy(
            src_ref=src, dst_ref=dst, send_sem=ssem.at[k],
            recv_sem=rsem.at[k] if recv is None else recv,
            device_id=peer, device_id_type=MESH,
        ).start()

    def await_bytes(ref, sem):
        pltpu.make_async_copy(ref, ref, sem).wait()

    me = x * NZ + z
    for m, b in ((0, bi), (1, bt)):
        loads[m].wait()
        w32 = wv[m].astype(F32)
        wtmp[...] = jnp.zeros_like(wtmp)
        for q in range(NS):
            @pl.when(s == q)
            def _(q=q, w32=w32):
                wtmp[:, :FFQ] = w32[:, q * FFQ:(q + 1) * FFQ]
        v = wtmp[...]
        brow = jnp.broadcast_to(b[...][None], (K8 + 1, b.shape[0]))
        pick = iota(brow.shape, 1) == blk * (K8 + 1) + iota(brow.shape, 0)
        bcol = jnp.sum(jnp.where(pick, brow, 0.0), axis=1, keepdims=True)
        hi = bcol.astype(BF).astype(F32)
        lo = (bcol - hi).astype(BF).astype(F32)
        lane = iota(v.shape, 1)
        v = jnp.where(lane == FFQ, hi, v)
        v = jnp.where(lane == FFQ + 1, lo, v)
        v = jnp.where(lane == FFQ + 2, bcol - hi - lo, v)
        wm[m, me] = v[:K8].astype(BF)
        wx[m, me] = v[K8:].astype(BF).astype(F32)

    rows = hv.shape[0]
    r8 = iota((8, rows), 0)
    t8 = iota((8, rows), 1)
    is_txt = s == 0
    at = (lax.shift_right_logical(t8, 6) == r8).astype(F32)
    ai = (r8 == s - 1).astype(F32)
    f_txt = is_txt.astype(F32)
    a = (f_txt * at + (1.0 - f_txt) * ai).astype(BF)
    scale = jnp.where(is_txt, 1.0 / TXT_LEN, 1.0 / rows)
    loads[2].wait()
    hsum = dot_nn(a, hv[...]) * scale
    hsend[...] = jnp.zeros_like(hsend)
    for q in range(NS):
        hsend[q, :, :FFQ] = hsum[:4, q * FFQ:(q + 1) * FFQ].astype(BF)
    hrecv[s] = hsend[s]
    n_m, n_e = NY * NZ * K8, NY * NZ
    c_m, c_e = iota((NY * NM, n_m), 1), iota((NE, n_e), 1)
    per_y, per_z = NZ * K8, NZ
    t_m = iota((NY * NM, n_m), 0) == c_m // per_y * NM + x * per_y + lax.rem(c_m, per_y)
    t_e = iota((NE, n_e), 0) == c_e // per_z * NZX + x * per_z + lax.rem(c_e, per_z)
    tm[...] = t_m.astype(F32).astype(BF)
    te[...] = t_e.astype(F32).astype(BF)
    xe[...] = jnp.zeros_like(xe)
    dls[...] = jnp.zeros_like(dls)

    pl.semaphore_wait(barrier, len(everyone))

    for d in range(1, NS):
        send(hsend.at[lax.rem(s + d, NS)], hrecv.at[s], 0, sect_peers[d - 1])
    def own_z(m):
        for i in range(NZ - 1):
            send(wm.at[m, me], wm.at[m, me], 1, z_peers[i], zsem.at[m, i, 0])
            send(wx.at[m, me], wx.at[m, me], 2, z_peers[i], zsem.at[m, i, 1])

    def own_x(m):
        for p in x_peers:
            send(wm.at[m, me], wm.at[m, me], 3 + 16 * m, p, xsem.at[m, 0])

    own_z(0)
    own_x(0)
    own_x(1)
    await_bytes(hrecv.at[pl.ds(0, NS - 1)], rsem.at[0])
    hr = hrecv[...].astype(F32)
    hq = jnp.concatenate([hr[0], hr[1] + hr[2] + hr[3]], axis=0)
    lane = iota(hq.shape, 1)
    ones = ((lane >= FFQ) & (lane < FFQ + 3)).astype(F32) * f_txt
    hall[y] = (hq + ones).astype(BF)
    for p in y_peers:
        send(hall.at[y], hall.at[y], 5, p)
    own_z(1)
    for m in range(2):
        for i in sorted(range(NZ - 1), key=lambda i: min(i + 1, NZ - 1 - i)):
            sl = x * NZ + lax.rem(z + NZ - (i + 1), NZ)
            await_bytes(wm.at[m, sl], zsem.at[m, i, 0])
            for p in x_peers:
                send(wm.at[m, sl], wm.at[m, sl], 3 + 16 * m, p, xsem.at[m, 0])
        for i in range(NZ - 1):
            sl = x * NZ + lax.rem(z + NZ - (i + 1), NZ)
            await_bytes(wx.at[m, sl], zsem.at[m, i, 1])
        four = wx.at[m, pl.ds(x * NZ, NZ)]
        for p in x_peers:
            send(four, four, 4 + 16 * m, p, xsem.at[m, 1])
    await_bytes(hall.at[pl.ds(0, NY - 1)], rsem.at[5])
    hrows = hall[...].reshape(NY * 8, LP)
    nx_in = (NX - 1) * NZ

    wf[y] = wm[1, pl.ds(x * NZ, NZ)].reshape(NZ * K8, LP)
    for j in range(NZ):
        we[y, j:j + 1, :] = wx[1, x * NZ + j]

    def ring_send(t):
        for k, far, hop in ((0, NY // 2, 1), (1, NY - 1 - NY // 2, NY - 1)):
            if t <= far:
                c = lax.rem(y + (NY - hop) * (t - 1), NY)
                p = {"blk_2": lax.rem(y + hop, NY)}
                send(wf.at[c], wf.at[c], 10 + k, p, ysem.at[k, t - 1, 0])
                send(we.at[c], we.at[c], 14 + k, p, ysem.at[k, t - 1, 1])

    def ring_wait(t):
        for k, far, hop in ((0, NY // 2, 1), (1, NY - 1 - NY // 2, NY - 1)):
            if t <= far:
                c = lax.rem(y + (NY - hop) * t, NY)
                await_bytes(wf.at[c], ysem.at[k, t - 1, 0])
                await_bytes(we.at[c], ysem.at[k, t - 1, 1])

    ring_send(1)

    def tile(m):
        await_bytes(wm.at[m, pl.ds(0, nx_in)], xsem.at[m, 0])
        await_bytes(wx.at[m, pl.ds(0, nx_in)], xsem.at[m, 1])
        for j in range(NZX):
            xpad[m, j:j + 1, :] = wx[m, j]
        xe[m, pl.ds(pl.multiple_of(y * NZX, NZX), NZX), :] = xpad[m].astype(BF)
        pe = dot_nt(hrows, xe[m])
        pm = dot_nt(hrows, wm[m].reshape(NM, LP))
        if m:
            for j in range(NY):
                ptx[j, :, :NM] = pm[8 * j:8 * j + 4]
                ptx[j, :, NM:] = pe[8 * j:8 * j + 4]
        else:
            pscr[:NY * 8] = pm
            pscr[NY * 8:] = pe
            for r in range(NT):
                psend[r, :, :NM] = pscr[pl.ds(4 + r, NY, stride=8), :]
                psend[r, :, NM:] = pscr[pl.ds(NY * 8 + 4 + r, NY, stride=8), :]

    tile(0)
    for d in range(1, NS):
        sp = lax.rem(s + d, NS)

        @pl.when(sp != 0)
        def _(d=d, sp=sp):
            send(psend.at[sp - 1], irecv.at[s], 6, sect_peers[d - 1])
    tile(1)
    for d in range(1, NS):
        sp = lax.rem(s + d, NS)

        @pl.when(sp == 0)
        def _(d=d):
            send(ptx, trecv.at[s], 7, sect_peers[d - 1])

    m_ = mult[0]
    n_dy = NX * (NS - 1)

    @pl.when(is_txt)
    def _():
        trecv[0] = ptx[...]
        await_bytes(trecv.at[pl.ds(0, NS - 1)], rsem.at[7])
        tsum[...] = jnp.sum(trecv[...], axis=0)
        tfull[y] = tsum[y]
        for d, p in zip(y_far, y_peers):
            send(tsum.at[lax.rem(y + d, NY)], tfull.at[y], 8, p)
        ring_wait(1)
        ring_send(2)
        await_bytes(tfull.at[pl.ds(0, NY - 1)], rsem.at[8])
        for j in range(NY):
            tbuf[:, j * NM:(j + 1) * NM] = tfull[j, :, :NM]
        tbuf[:, NY * NM:] = jnp.sum(tfull[:, :, NM:], axis=0)
        for i, p in enumerate(sect_peers):
            send(tbuf, tbuf, 16 + i, p, rsem.at[9])
        ring_wait(2)
        ring_send(3)
        ring_wait(3)
        ring_send(4)
        await_bytes(dyr, rsem.at[11])
        await_bytes(irecv.at[pl.ds(0, NS - 1)], ssem.at[6])
        await_bytes(tfull.at[pl.ds(0, NY - 1)], ssem.at[8])
        for i in range(NS - 1):
            await_bytes(tbuf, ssem.at[16 + i])

    @pl.when(jnp.logical_not(is_txt))
    def _():
        irecv[s] = psend[s - 1]
        await_bytes(irecv.at[pl.ds(0, NS - 1)], rsem.at[6])
        ifull[y] = jnp.sum(irecv[...], axis=0)
        for p in y_peers:
            send(ifull.at[y], ifull.at[y], 8, p)
        ring_wait(1)
        ring_send(2)
        await_bytes(ifull.at[pl.ds(0, NY - 1)], rsem.at[8])
        fv = ifull[...]
        extra = jnp.sum(fv[:, :, NM:], axis=0)
        unit, _ = unit_rows(jnp.concatenate([fv[j, :, :NM] for j in range(NY)] + [extra], axis=1))
        emb[zx] = unit.astype(BF)
        for p in zx_peers:
            send(emb.at[zx], emb.at[zx], 9, p, rsem.at[10])
        ring_wait(2)
        ring_send(3)
        NI = NZX * 8
        at_img = pos[0:NI]
        for j in range(1, NS - 1):
            at_img = jnp.where(s == j + 1, pos[j * NI:(j + 1) * NI], at_img)
        hit = at_img[None] == NT * blk + iota((4, NI), 0)
        label = jnp.where(hit, 1.0, -1.0)
        await_bytes(tbuf, rsem.at[9])
        t_unit, t_inv = unit_rows(tbuf[...])
        t_emb = t_unit.astype(BF)
        ring_wait(3)
        ring_send(4)
        await_bytes(emb.at[pl.ds(0, NZX - 1)], rsem.at[10])
        ev = emb[...].reshape(NI, NY * NM + NE)
        logits = m_ * dot_nt(t_emb, ev) + off[0]
        coef = -label * jax.nn.sigmoid(-label * logits)
        coef = jnp.where(iota(coef.shape, 0) < NT, coef, 0.0).astype(BF)
        g = m_ * dot_nn(coef, ev)
        gp = (g - t_unit * jnp.sum(t_unit * g, axis=-1, keepdims=True)) * t_inv
        slot = x * (NS - 1) + s - 1
        dyr[slot] = gp.astype(DY)
        for dx in x_far + [0]:
            for ds in range(NS):
                if dx or ds:
                    peer = {"sect": lax.rem(s + ds, NS), "blk_1": lax.rem(x + dx, NX)}
                    send(dyr.at[slot], dyr.at[slot], 13, peer, rsem.at[11])
        await_bytes(dyr.at[pl.ds(0, n_dy - 1)], rsem.at[11])
        await_bytes(ifull.at[pl.ds(0, NY - 1)], ssem.at[8])
        await_bytes(emb.at[pl.ds(0, NZX - 1)], ssem.at[9])
        await_bytes(emit.at[pl.ds(0, NX * NS - 1)], ssem.at[13])
        await_bytes(irecv.at[pl.ds(0, NS - 2)], ssem.at[6])
        await_bytes(ptx, ssem.at[7])

    for j in range(NX):
        v = sum(dyr[(NS - 1) * j + i].astype(F32) for i in range(NS - 1))
        dls[4 * j:4 * j + 4, :] = v
    dv = dls[...].astype(BF)
    d_m = dot_nn(dv[:, :NY * NM], tm[...]).astype(BF)
    d_e = dot_nn(dv[:, NY * NM:], te[...]).astype(BF)
    ring_wait(4)
    for j in range(NY):
        wes[NZ * j:NZ * (j + 1), :] = we[j]
    o = dot_nn(d_m, wf[...].reshape(n_m, LP)) + dot_nn(d_e, wes[...].astype(BF))
    for j in range(NX):
        osend[j] = o[4 * j:4 * j + 4].astype(OT)
    orecv[x] = osend[x]
    for d, p in zip(x_far, x_peers):
        send(osend.at[lax.rem(x + d, NX)], orecv.at[x], 12, p)
    await_bytes(orecv.at[pl.ds(0, NX - 1)], rsem.at[12])
    out[...] = jnp.sum(orecv[...].astype(F32), axis=0)[:NT, :FFQ]

    await_bytes(hrecv.at[pl.ds(0, NS - 1)], ssem.at[0])
    for k, ref in ((1, wm), (2, wx)):
        n_z = 2 * (NZ - 1)
        await_bytes(ref.at[0, pl.ds(0, n_z)], ssem.at[k])
    for k, ref in ((3, wm), (4, wx), (19, wm), (20, wx)):
        await_bytes(ref.at[0, pl.ds(0, nx_in)], ssem.at[k])
    for k, far in ((0, NY // 2), (1, NY - 1 - NY // 2)):
        await_bytes(wf.at[pl.ds(0, far)], ssem.at[10 + k])
        await_bytes(we.at[pl.ds(0, far)], ssem.at[14 + k])
    await_bytes(hall.at[pl.ds(0, NY - 1)], ssem.at[5])
    await_bytes(orecv.at[pl.ds(0, NX - 1)], ssem.at[12])


def on_device(hidden, w_txt, w_img, b_txt, b_img, mult, off, pos):
    NS, NZ, NX, NY = (lax.axis_size(a) for a in SECT_BLK)
    _, rows, FF = hidden.shape
    D = b_txt.shape[0]
    K = w_txt.shape[1]
    NZX = NZ * NX
    NM, NE = NZX * K8, NZX * NY
    FFQ = FF // NS
    LP = (FFQ + 3 + 127) // 128 * 128
    dims = (NS, NZ, NX, NY, FF)
    vm = pltpu.VMEM
    scratch = [
        vm((rows, FF), BF),
        vm((2, K, FF), BF),
        vm((K, LP), F32),
        vm((2, NZX, K8, LP), BF),
        vm((2, NZX, 1, LP), F32),
        vm((2, NZX, LP), F32),
        vm((NS, 4, LP), BF),
        vm((NS, 4, LP), BF),
        vm((NY, 8, LP), BF),
        vm((2, NE, LP), BF),
        vm((2 * NY * 8, NM), F32),
        vm((NT, NY, NM + NE), F32),
        vm((NY, 4, NM + NE), F32),
        vm((NS, NY, NM + NE), F32),
        vm((NS, NY, 4, NM + NE), F32),
        vm((NY, NY, NM + NE), F32),
        vm((NY, 4, NM + NE), F32),
        vm((NY, 4, NM + NE), F32),
        vm((4, D), F32),
        vm((NZX, 8, D), BF),
        vm((NX * NS, 4, D), DY),
        vm((NX * (NS - 1), 4, D), DY),
        vm((NX * 4, D), F32),
        vm((NX, 4, LP), OT),
        vm((NX, 4, LP), OT),
        vm((NY, NZ * K8, LP), BF),
        vm((NY, NZ, LP), F32),
        vm((NY * NZ, LP), F32),
        vm((NY * NM, NY * NZ * K8), BF),
        vm((NE, NY * NZ), BF),
        pltpu.SemaphoreType.DMA((3,)),
        pltpu.SemaphoreType.DMA((21,)),
        pltpu.SemaphoreType.DMA((13,)),
        pltpu.SemaphoreType.DMA((2, NZ - 1, 2)),
        pltpu.SemaphoreType.DMA((2, 2)),
        pltpu.SemaphoreType.DMA((2, NY // 2, 2)),
    ]
    any_ = pl.BlockSpec(memory_space=pl.ANY)
    vmem = pl.BlockSpec(memory_space=pltpu.VMEM)
    smem = pl.BlockSpec(memory_space=pltpu.SMEM)
    return pl.pallas_call(
        functools.partial(kernel, dims),
        out_shape=jax.ShapeDtypeStruct((NT, FFQ), F32),
        in_specs=[any_, any_, any_, vmem, vmem, smem, smem, vmem],
        out_specs=vmem,
        scratch_shapes=scratch,
        compiler_params=pltpu.CompilerParams(collective_id=0, has_side_effects=True),
    )(
        hidden[0], w_txt.T, w_img.T, b_txt, b_img, mult, off, pos
    )


def solution(mesh):
    finer = Mesh(
        mesh.devices.reshape(mesh.shape["sect"], 4, 4, 8), ("sect", "blk_0", "blk_1", "blk_2")
    )
    placed = (P(SECT_BLK, None, None), P(None, BLK), P(None, BLK), P(), P(), P(), P(), P())
    return jax.shard_map(
        on_device, mesh=finer, in_specs=placed, out_specs=P(BLK, "sect"), check_vma=False
    )
```

```python
import functools

import jax
import jax.numpy as jnp
from jax import lax
from jax.experimental import pallas as pl
from jax.experimental.pallas import tpu as pltpu
from jax.sharding import Mesh
from jax.sharding import PartitionSpec as P

TXT_LEN = 64
NT = 3
K8 = 8
BF = jnp.bfloat16
F32 = jnp.float32
BLK = ("blk_0", "blk_1", "blk_2")
SECT_BLK = ("sect", "blk_0", "blk_1", "blk_2")
MESH = pl.DeviceIdType.MESH
DY = F32
OT = F32


def iota(shape, dim):
    return lax.broadcasted_iota(jnp.int32, shape, dim)


def dot_nn(a, b):
    return lax.dot_general(a, b, (((1,), (0,)), ((), ())), preferred_element_type=F32)


def dot_nt(a, b):
    return lax.dot_general(a, b, (((1,), (1,)), ((), ())), preferred_element_type=F32)


def unit_rows(p):
    inv = lax.rsqrt(jnp.sum(p * p, axis=-1, keepdims=True) + 1e-06)
    return p * inv, inv


def kernel(
    dims,
    hid, wt, wi, bt_hbm, bi_hbm, mult, off, pos_hbm,
    out,
    hv, wv, wtmp, wm, wx, xpad,
    hsend, hrecv, hall,
    xe, pscr, psend, ptx, irecv, trecv, ifull, tsum, tfull,
    tbuf, emb, emit, dyr, dls, osend, orecv,
    wf, we, wes, tm, te,
    bt, bi, pos, lsem, ssem, rsem, zsem, xsem, ysem,
):
    NS, NZ, NX, NY, FF = dims
    FFQ = FF // NS
    LP = wtmp.shape[1]
    NZX = NZ * NX
    NM = NZX * K8
    NE = NZX * NY
    s = lax.axis_index("sect")
    z = lax.axis_index("blk_0")
    x = lax.axis_index("blk_1")
    y = lax.axis_index("blk_2")
    zx = z * NX + x
    blk = zx * NY + y

    sect_peers = [{"sect": lax.rem(s + d, NS)} for d in range(1, NS)]
    y_far = sorted(range(1, NY), key=lambda d: -min(d, NY - d))
    y_peers = [{"blk_2": lax.rem(y + d, NY)} for d in y_far]
    z_peers = [{"blk_0": lax.rem(z + d, NZ)} for d in range(1, NZ)]
    x_far = sorted(range(1, NX), key=lambda d: -min(d, NX - d))
    x_peers = [{"blk_1": lax.rem(x + d, NX)} for d in x_far]
    zx_peers = []
    far = [(dz, dx) for dz in range(NZ) for dx in range(NX)][1:]
    far = sorted(far, key=lambda d: -2 * min(d[0], NZ - d[0]) - min(d[1], NX - d[1]))
    for dz, dx in far:
        zx_peers.append({"blk_0": lax.rem(z + dz, NZ), "blk_1": lax.rem(x + dx, NX)})

    loads = [
        pltpu.make_async_copy(wi, wv.at[0], lsem.at[0]),
        pltpu.make_async_copy(wt, wv.at[1], lsem.at[1]),
        pltpu.make_async_copy(hid, hv, lsem.at[2]),
        pltpu.make_async_copy(bi_hbm, bi, lsem.at[3]),
        pltpu.make_async_copy(bt_hbm, bt, lsem.at[4]),
        pltpu.make_async_copy(pos_hbm, pos, lsem.at[5]),
    ]
    for c in loads:
        c.start()
    barrier = pltpu.get_barrier_semaphore()
    everyone = sect_peers + y_peers + x_peers + z_peers
    for p in everyone:
        pl.semaphore_signal(barrier, inc=1, device_id=p, device_id_type=MESH)

    def send(src, dst, k, peer, recv=None):
        pltpu.make_async_remote_copy(
            src_ref=src, dst_ref=dst, send_sem=ssem.at[k],
            recv_sem=rsem.at[k] if recv is None else recv,
            device_id=peer, device_id_type=MESH,
        ).start()

    def await_bytes(ref, sem):
        pltpu.make_async_copy(ref, ref, sem).wait()

    me = x * NZ + z
    for m, b in ((0, bi), (1, bt)):
        loads[m].wait()
        loads[3 + m].wait()
        w32 = wv[m].astype(F32)
        wtmp[...] = jnp.zeros_like(wtmp)
        for q in range(NS):
            @pl.when(s == q)
            def _(q=q, w32=w32):
                wtmp[:, :FFQ] = w32[:, q * FFQ:(q + 1) * FFQ]
        v = wtmp[...]
        brow = jnp.broadcast_to(b[...][None], (K8 + 1, b.shape[0]))
        pick = iota(brow.shape, 1) == blk * (K8 + 1) + iota(brow.shape, 0)
        bcol = jnp.sum(jnp.where(pick, brow, 0.0), axis=1, keepdims=True)
        hi = bcol.astype(BF).astype(F32)
        lo = (bcol - hi).astype(BF).astype(F32)
        lane = iota(v.shape, 1)
        v = jnp.where(lane == FFQ, hi, v)
        v = jnp.where(lane == FFQ + 1, lo, v)
        v = jnp.where(lane == FFQ + 2, bcol - hi - lo, v)
        wm[m, me] = v[:K8].astype(BF)
        wx[m, me] = v[K8:].astype(BF).astype(F32)

    rows = hv.shape[0]
    r8 = iota((8, rows), 0)
    t8 = iota((8, rows), 1)
    is_txt = s == 0
    at = (lax.shift_right_logical(t8, 6) == r8).astype(F32)
    ai = (r8 == s - 1).astype(F32)
    f_txt = is_txt.astype(F32)
    a = (f_txt * at + (1.0 - f_txt) * ai).astype(BF)
    scale = jnp.where(is_txt, 1.0 / TXT_LEN, 1.0 / rows)
    loads[2].wait()
    loads[5].wait()
    hsum = dot_nn(a, hv[...]) * scale
    hsend[...] = jnp.zeros_like(hsend)
    for q in range(NS):
        hsend[q, :, :FFQ] = hsum[:4, q * FFQ:(q + 1) * FFQ].astype(BF)
    hrecv[s] = hsend[s]
    n_m, n_e = NY * NZ * K8, NY * NZ
    c_m, c_e = iota((NY * NM, n_m), 1), iota((NE, n_e), 1)
    per_y, per_z = NZ * K8, NZ
    t_m = iota((NY * NM, n_m), 0) == c_m // per_y * NM + x * per_y + lax.rem(c_m, per_y)
    t_e = iota((NE, n_e), 0) == c_e // per_z * NZX + x * per_z + lax.rem(c_e, per_z)
    tm[...] = t_m.astype(F32).astype(BF)
    te[...] = t_e.astype(F32).astype(BF)
    xe[...] = jnp.zeros_like(xe)
    dls[...] = jnp.zeros_like(dls)

    pl.semaphore_wait(barrier, len(everyone))

    for d in range(1, NS):
        send(hsend.at[lax.rem(s + d, NS)], hrecv.at[s], 0, sect_peers[d - 1])
    def own_z(m):
        for i in range(NZ - 1):
            send(wm.at[m, me], wm.at[m, me], 1, z_peers[i], zsem.at[m, i, 0])
            send(wx.at[m, me], wx.at[m, me], 2, z_peers[i], zsem.at[m, i, 1])

    def own_x(m):
        for p in x_peers:
            send(wm.at[m, me], wm.at[m, me], 3 + 16 * m, p, xsem.at[m, 0])

    own_z(0)
    own_x(0)
    own_x(1)
    await_bytes(hrecv.at[pl.ds(0, NS - 1)], rsem.at[0])
    hr = hrecv[...].astype(F32)
    hq = jnp.concatenate([hr[0], hr[1] + hr[2] + hr[3]], axis=0)
    lane = iota(hq.shape, 1)
    ones = ((lane >= FFQ) & (lane < FFQ + 3)).astype(F32) * f_txt
    hall[y] = (hq + ones).astype(BF)
    for p in y_peers:
        send(hall.at[y], hall.at[y], 5, p)
    own_z(1)
    for m in range(2):
        for i in sorted(range(NZ - 1), key=lambda i: min(i + 1, NZ - 1 - i)):
            sl = x * NZ + lax.rem(z + NZ - (i + 1), NZ)
            await_bytes(wm.at[m, sl], zsem.at[m, i, 0])
            for p in x_peers:
                send(wm.at[m, sl], wm.at[m, sl], 3 + 16 * m, p, xsem.at[m, 0])
        for i in range(NZ - 1):
            sl = x * NZ + lax.rem(z + NZ - (i + 1), NZ)
            await_bytes(wx.at[m, sl], zsem.at[m, i, 1])
        four = wx.at[m, pl.ds(x * NZ, NZ)]
        for p in x_peers:
            send(four, four, 4 + 16 * m, p, xsem.at[m, 1])
    await_bytes(hall.at[pl.ds(0, NY - 1)], rsem.at[5])
    hrows = hall[...].reshape(NY * 8, LP)
    nx_in = (NX - 1) * NZ

    wf[y] = wm[1, pl.ds(x * NZ, NZ)].reshape(NZ * K8, LP)
    for j in range(NZ):
        we[y, j:j + 1, :] = wx[1, x * NZ + j]

    def ring_send(t):
        for k, far, hop in ((0, NY // 2, 1), (1, NY - 1 - NY // 2, NY - 1)):
            if t <= far:
                c = lax.rem(y + (NY - hop) * (t - 1), NY)
                p = {"blk_2": lax.rem(y + hop, NY)}
                send(wf.at[c], wf.at[c], 10 + k, p, ysem.at[k, t - 1, 0])
                send(we.at[c], we.at[c], 14 + k, p, ysem.at[k, t - 1, 1])

    def ring_wait(t):
        for k, far, hop in ((0, NY // 2, 1), (1, NY - 1 - NY // 2, NY - 1)):
            if t <= far:
                c = lax.rem(y + (NY - hop) * t, NY)
                await_bytes(wf.at[c], ysem.at[k, t - 1, 0])
                await_bytes(we.at[c], ysem.at[k, t - 1, 1])

    ring_send(1)

    def tile(m):
        await_bytes(wm.at[m, pl.ds(0, nx_in)], xsem.at[m, 0])
        await_bytes(wx.at[m, pl.ds(0, nx_in)], xsem.at[m, 1])
        for j in range(NZX):
            xpad[m, j:j + 1, :] = wx[m, j]
        xe[m, pl.ds(pl.multiple_of(y * NZX, NZX), NZX), :] = xpad[m].astype(BF)
        pe = dot_nt(hrows, xe[m])
        pm = dot_nt(hrows, wm[m].reshape(NM, LP))
        if m:
            for j in range(NY):
                ptx[j, :, :NM] = pm[8 * j:8 * j + 4]
                ptx[j, :, NM:] = pe[8 * j:8 * j + 4]
        else:
            pscr[:NY * 8] = pm
            pscr[NY * 8:] = pe
            for r in range(NT):
                psend[r, :, :NM] = pscr[pl.ds(4 + r, NY, stride=8), :]
                psend[r, :, NM:] = pscr[pl.ds(NY * 8 + 4 + r, NY, stride=8), :]

    tile(0)
    for d in range(1, NS):
        sp = lax.rem(s + d, NS)

        @pl.when(sp != 0)
        def _(d=d, sp=sp):
            send(psend.at[sp - 1], irecv.at[s], 6, sect_peers[d - 1])
    tile(1)
    for d in range(1, NS):
        sp = lax.rem(s + d, NS)

        @pl.when(sp == 0)
        def _(d=d):
            send(ptx, trecv.at[s], 7, sect_peers[d - 1])

    m_ = mult[0]
    n_dy = NX * (NS - 1)

    @pl.when(is_txt)
    def _():
        trecv[0] = ptx[...]
        await_bytes(trecv.at[pl.ds(0, NS - 1)], rsem.at[7])
        tsum[...] = jnp.sum(trecv[...], axis=0)
        tfull[y] = tsum[y]
        for d, p in zip(y_far, y_peers):
            send(tsum.at[lax.rem(y + d, NY)], tfull.at[y], 8, p)
        ring_wait(1)
        ring_send(2)
        await_bytes(tfull.at[pl.ds(0, NY - 1)], rsem.at[8])
        for j in range(NY):
            tbuf[:, j * NM:(j + 1) * NM] = tfull[j, :, :NM]
        tbuf[:, NY * NM:] = jnp.sum(tfull[:, :, NM:], axis=0)
        for i, p in enumerate(sect_peers):
            send(tbuf, tbuf, 16 + i, p, rsem.at[9])
        ring_wait(2)
        ring_send(3)
        ring_wait(3)
        ring_send(4)
        await_bytes(dyr, rsem.at[11])
        await_bytes(irecv.at[pl.ds(0, NS - 1)], ssem.at[6])
        await_bytes(tfull.at[pl.ds(0, NY - 1)], ssem.at[8])
        for i in range(NS - 1):
            await_bytes(tbuf, ssem.at[16 + i])

    @pl.when(jnp.logical_not(is_txt))
    def _():
        irecv[s] = psend[s - 1]
        await_bytes(irecv.at[pl.ds(0, NS - 1)], rsem.at[6])
        ifull[y] = jnp.sum(irecv[...], axis=0)
        for p in y_peers:
            send(ifull.at[y], ifull.at[y], 8, p)
        ring_wait(1)
        ring_send(2)
        await_bytes(ifull.at[pl.ds(0, NY - 1)], rsem.at[8])
        fv = ifull[...]
        extra = jnp.sum(fv[:, :, NM:], axis=0)
        unit, _ = unit_rows(jnp.concatenate([fv[j, :, :NM] for j in range(NY)] + [extra], axis=1))
        emb[zx] = unit.astype(BF)
        for p in zx_peers:
            send(emb.at[zx], emb.at[zx], 9, p, rsem.at[10])
        ring_wait(2)
        ring_send(3)
        NI = NZX * 8
        at_img = pos[0:NI]
        for j in range(1, NS - 1):
            at_img = jnp.where(s == j + 1, pos[j * NI:(j + 1) * NI], at_img)
        hit = at_img[None] == NT * blk + iota((4, NI), 0)
        label = jnp.where(hit, 1.0, -1.0)
        await_bytes(tbuf, rsem.at[9])
        t_unit, t_inv = unit_rows(tbuf[...])
        t_emb = t_unit.astype(BF)
        ring_wait(3)
        ring_send(4)
        await_bytes(emb.at[pl.ds(0, NZX - 1)], rsem.at[10])
        ev = emb[...].reshape(NI, NY * NM + NE)
        logits = m_ * dot_nt(t_emb, ev) + off[0]
        coef = -label * jax.nn.sigmoid(-label * logits)
        coef = jnp.where(iota(coef.shape, 0) < NT, coef, 0.0).astype(BF)
        g = m_ * dot_nn(coef, ev)
        gp = (g - t_unit * jnp.sum(t_unit * g, axis=-1, keepdims=True)) * t_inv
        slot = x * (NS - 1) + s - 1
        dyr[slot] = gp.astype(DY)
        for dx in x_far + [0]:
            for ds in range(NS):
                if dx or ds:
                    peer = {"sect": lax.rem(s + ds, NS), "blk_1": lax.rem(x + dx, NX)}
                    send(dyr.at[slot], dyr.at[slot], 13, peer, rsem.at[11])
        await_bytes(dyr.at[pl.ds(0, n_dy - 1)], rsem.at[11])
        await_bytes(ifull.at[pl.ds(0, NY - 1)], ssem.at[8])
        await_bytes(emb.at[pl.ds(0, NZX - 1)], ssem.at[9])
        await_bytes(emit.at[pl.ds(0, NX * NS - 1)], ssem.at[13])
        await_bytes(irecv.at[pl.ds(0, NS - 2)], ssem.at[6])
        await_bytes(ptx, ssem.at[7])

    for j in range(NX):
        v = sum(dyr[(NS - 1) * j + i].astype(F32) for i in range(NS - 1))
        dls[4 * j:4 * j + 4, :] = v
    dv = dls[...].astype(BF)
    d_m = dot_nn(dv[:, :NY * NM], tm[...]).astype(BF)
    d_e = dot_nn(dv[:, NY * NM:], te[...]).astype(BF)
    ring_wait(4)
    for j in range(NY):
        wes[NZ * j:NZ * (j + 1), :] = we[j]
    o = dot_nn(d_m, wf[...].reshape(n_m, LP)) + dot_nn(d_e, wes[...].astype(BF))
    for j in range(NX):
        osend[j] = o[4 * j:4 * j + 4].astype(OT)
    orecv[x] = osend[x]
    for d, p in zip(x_far, x_peers):
        send(osend.at[lax.rem(x + d, NX)], orecv.at[x], 12, p)
    await_bytes(orecv.at[pl.ds(0, NX - 1)], rsem.at[12])
    out[...] = jnp.sum(orecv[...].astype(F32), axis=0)[:NT, :FFQ]

    await_bytes(hrecv.at[pl.ds(0, NS - 1)], ssem.at[0])
    for k, ref in ((1, wm), (2, wx)):
        n_z = 2 * (NZ - 1)
        await_bytes(ref.at[0, pl.ds(0, n_z)], ssem.at[k])
    for k, ref in ((3, wm), (4, wx), (19, wm), (20, wx)):
        await_bytes(ref.at[0, pl.ds(0, nx_in)], ssem.at[k])
    for k, far in ((0, NY // 2), (1, NY - 1 - NY // 2)):
        await_bytes(wf.at[pl.ds(0, far)], ssem.at[10 + k])
        await_bytes(we.at[pl.ds(0, far)], ssem.at[14 + k])
    await_bytes(hall.at[pl.ds(0, NY - 1)], ssem.at[5])
    await_bytes(orecv.at[pl.ds(0, NX - 1)], ssem.at[12])


def on_device(hidden, w_txt, w_img, b_txt, b_img, mult, off, pos):
    NS, NZ, NX, NY = (lax.axis_size(a) for a in SECT_BLK)
    _, rows, FF = hidden.shape
    D = b_txt.shape[0]
    K = w_txt.shape[1]
    NZX = NZ * NX
    NM, NE = NZX * K8, NZX * NY
    FFQ = FF // NS
    LP = (FFQ + 3 + 127) // 128 * 128
    dims = (NS, NZ, NX, NY, FF)
    vm = pltpu.VMEM
    scratch = [
        vm((rows, FF), BF),
        vm((2, K, FF), BF),
        vm((K, LP), F32),
        vm((2, NZX, K8, LP), BF),
        vm((2, NZX, 1, LP), F32),
        vm((2, NZX, LP), F32),
        vm((NS, 4, LP), BF),
        vm((NS, 4, LP), BF),
        vm((NY, 8, LP), BF),
        vm((2, NE, LP), BF),
        vm((2 * NY * 8, NM), F32),
        vm((NT, NY, NM + NE), F32),
        vm((NY, 4, NM + NE), F32),
        vm((NS, NY, NM + NE), F32),
        vm((NS, NY, 4, NM + NE), F32),
        vm((NY, NY, NM + NE), F32),
        vm((NY, 4, NM + NE), F32),
        vm((NY, 4, NM + NE), F32),
        vm((4, D), F32),
        vm((NZX, 8, D), BF),
        vm((NX * NS, 4, D), DY),
        vm((NX * (NS - 1), 4, D), DY),
        vm((NX * 4, D), F32),
        vm((NX, 4, LP), OT),
        vm((NX, 4, LP), OT),
        vm((NY, NZ * K8, LP), BF),
        vm((NY, NZ, LP), F32),
        vm((NY * NZ, LP), F32),
        vm((NY * NM, NY * NZ * K8), BF),
        vm((NE, NY * NZ), BF),
        vm((D,), F32),
        vm((D,), F32),
        vm(pos.shape, jnp.int32),
        pltpu.SemaphoreType.DMA((6,)),
        pltpu.SemaphoreType.DMA((21,)),
        pltpu.SemaphoreType.DMA((13,)),
        pltpu.SemaphoreType.DMA((2, NZ - 1, 2)),
        pltpu.SemaphoreType.DMA((2, 2)),
        pltpu.SemaphoreType.DMA((2, NY // 2, 2)),
    ]
    any_ = pl.BlockSpec(memory_space=pl.ANY)
    vmem = pl.BlockSpec(memory_space=pltpu.VMEM)
    smem = pl.BlockSpec(memory_space=pltpu.SMEM)
    return pl.pallas_call(
        functools.partial(kernel, dims),
        out_shape=pltpu.VMEM((NT, FFQ), F32),
        in_specs=[any_, any_, any_, any_, any_, smem, smem, any_],
        out_specs=vmem,
        scratch_shapes=scratch,
        compiler_params=pltpu.CompilerParams(collective_id=0, has_side_effects=True),
    )(
        hidden[0], w_txt.T, w_img.T, b_txt, b_img, mult, off, pos
    )


def solution(mesh):
    finer = Mesh(
        mesh.devices.reshape(mesh.shape["sect"], 4, 4, 8), ("sect", "blk_0", "blk_1", "blk_2")
    )
    placed = (P(SECT_BLK, None, None), P(None, BLK), P(None, BLK), P(), P(), P(), P(), P())
    return jax.shard_map(
        on_device, mesh=finer, in_specs=placed, out_specs=P(BLK, "sect"), check_vma=False
    )
```

```python
import functools

import jax
import jax.numpy as jnp
from jax import lax
from jax.experimental import pallas as pl
from jax.experimental.pallas import tpu as pltpu
from jax.sharding import Mesh
from jax.sharding import PartitionSpec as P

TXT_LEN = 64
NT = 3
K8 = 8
BF = jnp.bfloat16
F32 = jnp.float32
BLK = ("blk_0", "blk_1", "blk_2")
SECT_BLK = ("sect", "blk_0", "blk_1", "blk_2")
MESH = pl.DeviceIdType.MESH
DY = F32
OT = F32


def iota(shape, dim):
    return lax.broadcasted_iota(jnp.int32, shape, dim)


def dot_nn(a, b):
    return lax.dot_general(a, b, (((1,), (0,)), ((), ())), preferred_element_type=F32)


def dot_nt(a, b):
    return lax.dot_general(a, b, (((1,), (1,)), ((), ())), preferred_element_type=F32)


def unit_rows(p):
    inv = lax.rsqrt(jnp.sum(p * p, axis=-1, keepdims=True) + 1e-06)
    return p * inv, inv


def kernel(
    dims,
    hid, wt, wi, bt_hbm, bi_hbm, mult, off, pos_hbm,
    out,
    hv, wv, wtmp, wm, wx, xpad,
    hsend, hrecv, hall,
    xe, pscr, psend, ptx, irecv, trecv, ifull, tsum, tfull,
    tbuf, emb, emit, dyr, dls, osend, orecv,
    wf, we, wes,
    bt, bi, pos, lsem, ssem, rsem, zsem, xsem, ysem,
):
    NS, NZ, NX, NY, FF = dims
    FFQ = FF // NS
    LP = wtmp.shape[1]
    NZX = NZ * NX
    NM = NZX * K8
    NE = NZX * NY
    s = lax.axis_index("sect")
    z = lax.axis_index("blk_0")
    x = lax.axis_index("blk_1")
    y = lax.axis_index("blk_2")
    zx = z * NX + x
    blk = zx * NY + y

    sect_peers = [{"sect": lax.rem(s + d, NS)} for d in range(1, NS)]
    y_far = sorted(range(1, NY), key=lambda d: -min(d, NY - d))
    y_peers = [{"blk_2": lax.rem(y + d, NY)} for d in y_far]
    z_peers = [{"blk_0": lax.rem(z + d, NZ)} for d in range(1, NZ)]
    x_far = sorted(range(1, NX), key=lambda d: -min(d, NX - d))
    x_peers = [{"blk_1": lax.rem(x + d, NX)} for d in x_far]
    zx_peers = []
    far = [(dz, dx) for dz in range(NZ) for dx in range(NX)][1:]
    far = sorted(far, key=lambda d: -2 * min(d[0], NZ - d[0]) - min(d[1], NX - d[1]))
    for dz, dx in far:
        zx_peers.append({"blk_0": lax.rem(z + dz, NZ), "blk_1": lax.rem(x + dx, NX)})

    loads = [
        pltpu.make_async_copy(wi, wv.at[0], lsem.at[0]),
        pltpu.make_async_copy(wt, wv.at[1], lsem.at[1]),
        pltpu.make_async_copy(hid, hv, lsem.at[2]),
        pltpu.make_async_copy(bi_hbm, bi, lsem.at[3]),
        pltpu.make_async_copy(bt_hbm, bt, lsem.at[4]),
        pltpu.make_async_copy(pos_hbm, pos, lsem.at[5]),
    ]
    for c in loads:
        c.start()
    barrier = pltpu.get_barrier_semaphore()
    everyone = sect_peers + y_peers + x_peers + z_peers
    for p in everyone:
        pl.semaphore_signal(barrier, inc=1, device_id=p, device_id_type=MESH)

    def send(src, dst, k, peer, recv=None):
        pltpu.make_async_remote_copy(
            src_ref=src, dst_ref=dst, send_sem=ssem.at[k],
            recv_sem=rsem.at[k] if recv is None else recv,
            device_id=peer, device_id_type=MESH,
        ).start()

    def await_bytes(ref, sem):
        pltpu.make_async_copy(ref, ref, sem).wait()

    me = x * NZ + z
    for m, b in ((0, bi), (1, bt)):
        loads[m].wait()
        loads[3 + m].wait()
        w32 = wv[m].astype(F32)
        wtmp[...] = jnp.zeros_like(wtmp)
        for q in range(NS):
            @pl.when(s == q)
            def _(q=q, w32=w32):
                wtmp[:, :FFQ] = w32[:, q * FFQ:(q + 1) * FFQ]
        v = wtmp[...]
        brow = jnp.broadcast_to(b[...][None], (K8 + 1, b.shape[0]))
        pick = iota(brow.shape, 1) == blk * (K8 + 1) + iota(brow.shape, 0)
        bcol = jnp.sum(jnp.where(pick, brow, 0.0), axis=1, keepdims=True)
        hi = bcol.astype(BF).astype(F32)
        lo = (bcol - hi).astype(BF).astype(F32)
        lane = iota(v.shape, 1)
        v = jnp.where(lane == FFQ, hi, v)
        v = jnp.where(lane == FFQ + 1, lo, v)
        v = jnp.where(lane == FFQ + 2, bcol - hi - lo, v)
        wm[m, me] = v[:K8].astype(BF)
        wx[m, me] = v[K8:].astype(BF).astype(F32)

    rows = hv.shape[0]
    r8 = iota((8, rows), 0)
    t8 = iota((8, rows), 1)
    is_txt = s == 0
    at = (lax.shift_right_logical(t8, 6) == r8).astype(F32)
    ai = (r8 == s - 1).astype(F32)
    f_txt = is_txt.astype(F32)
    a = (f_txt * at + (1.0 - f_txt) * ai).astype(BF)
    scale = jnp.where(is_txt, 1.0 / TXT_LEN, 1.0 / rows)
    loads[2].wait()
    loads[5].wait()
    hsum = dot_nn(a, hv[...]) * scale
    hsend[...] = jnp.zeros_like(hsend)
    for q in range(NS):
        hsend[q, :, :FFQ] = hsum[:4, q * FFQ:(q + 1) * FFQ].astype(BF)
    hrecv[s] = hsend[s]
    xe[...] = jnp.zeros_like(xe)
    dls[...] = jnp.zeros_like(dls)

    pl.semaphore_wait(barrier, len(everyone))

    for d in range(1, NS):
        send(hsend.at[lax.rem(s + d, NS)], hrecv.at[s], 0, sect_peers[d - 1])
    def own_z(m):
        for i in range(NZ - 1):
            send(wm.at[m, me], wm.at[m, me], 1, z_peers[i], zsem.at[m, i, 0])
            send(wx.at[m, me], wx.at[m, me], 2, z_peers[i], zsem.at[m, i, 1])

    def own_x(m):
        for p in x_peers:
            send(wm.at[m, me], wm.at[m, me], 3 + 16 * m, p, xsem.at[m, 0])

    own_z(0)
    own_x(0)
    own_x(1)
    await_bytes(hrecv.at[pl.ds(0, NS - 1)], rsem.at[0])
    hr = hrecv[...].astype(F32)
    hq = jnp.concatenate([hr[0], hr[1] + hr[2] + hr[3]], axis=0)
    lane = iota(hq.shape, 1)
    ones = ((lane >= FFQ) & (lane < FFQ + 3)).astype(F32) * f_txt
    hall[y] = (hq + ones).astype(BF)
    for p in y_peers:
        send(hall.at[y], hall.at[y], 5, p)
    own_z(1)
    for m in range(2):
        for i in sorted(range(NZ - 1), key=lambda i: min(i + 1, NZ - 1 - i)):
            sl = x * NZ + lax.rem(z + NZ - (i + 1), NZ)
            await_bytes(wm.at[m, sl], zsem.at[m, i, 0])
            for p in x_peers:
                send(wm.at[m, sl], wm.at[m, sl], 3 + 16 * m, p, xsem.at[m, 0])
        for i in range(NZ - 1):
            sl = x * NZ + lax.rem(z + NZ - (i + 1), NZ)
            await_bytes(wx.at[m, sl], zsem.at[m, i, 1])
        four = wx.at[m, pl.ds(x * NZ, NZ)]
        for p in x_peers:
            send(four, four, 4 + 16 * m, p, xsem.at[m, 1])
    await_bytes(hall.at[pl.ds(0, NY - 1)], rsem.at[5])
    hrows = hall[...].reshape(NY * 8, LP)
    nx_in = (NX - 1) * NZ

    wf[y] = wm[1, pl.ds(x * NZ, NZ)].reshape(NZ * K8, LP)
    for j in range(NZ):
        we[y, j:j + 1, :] = wx[1, x * NZ + j]

    def ring_send(t):
        for k, far, hop in ((0, NY // 2, 1), (1, NY - 1 - NY // 2, NY - 1)):
            if t <= far:
                c = lax.rem(y + (NY - hop) * (t - 1), NY)
                p = {"blk_2": lax.rem(y + hop, NY)}
                send(wf.at[c], wf.at[c], 10 + k, p, ysem.at[k, t - 1, 0])
                send(we.at[c], we.at[c], 14 + k, p, ysem.at[k, t - 1, 1])

    def ring_wait(t):
        for k, far, hop in ((0, NY // 2, 1), (1, NY - 1 - NY // 2, NY - 1)):
            if t <= far:
                c = lax.rem(y + (NY - hop) * t, NY)
                await_bytes(wf.at[c], ysem.at[k, t - 1, 0])
                await_bytes(we.at[c], ysem.at[k, t - 1, 1])

    ring_send(1)

    def tile(m):
        await_bytes(wm.at[m, pl.ds(0, nx_in)], xsem.at[m, 0])
        await_bytes(wx.at[m, pl.ds(0, nx_in)], xsem.at[m, 1])
        for j in range(NZX):
            xpad[m, j:j + 1, :] = wx[m, j]
        xe[m, pl.ds(pl.multiple_of(y * NZX, NZX), NZX), :] = xpad[m].astype(BF)
        pe = dot_nt(hrows, xe[m])
        pm = dot_nt(hrows, wm[m].reshape(NM, LP))
        if m:
            for j in range(NY):
                ptx[j, :, :NM] = pm[8 * j:8 * j + 4]
                ptx[j, :, NM:] = pe[8 * j:8 * j + 4]
        else:
            pscr[:NY * 8] = pm
            pscr[NY * 8:2 * NY * 8] = pe
            for r in range(NT):
                psend[r, :, :NM] = pscr[pl.ds(4 + r, NY, stride=8), :]
                psend[r, :, NM:] = pscr[pl.ds(NY * 8 + 4 + r, NY, stride=8), :]

    tile(0)
    for d in range(1, NS):
        sp = lax.rem(s + d, NS)

        @pl.when(sp != 0)
        def _(d=d, sp=sp):
            send(psend.at[sp - 1], irecv.at[s], 6, sect_peers[d - 1])
    tile(1)
    for d in range(1, NS):
        sp = lax.rem(s + d, NS)

        @pl.when(sp == 0)
        def _(d=d):
            send(ptx, trecv.at[s], 7, sect_peers[d - 1])

    m_ = mult[0]
    n_dy = NX * (NS - 1)

    @pl.when(is_txt)
    def _():
        trecv[0] = ptx[...]
        await_bytes(trecv.at[pl.ds(0, NS - 1)], rsem.at[7])
        tsum[...] = jnp.sum(trecv[...], axis=0)
        tfull[y] = tsum[y]
        for d, p in zip(y_far, y_peers):
            send(tsum.at[lax.rem(y + d, NY)], tfull.at[y], 8, p)
        ring_wait(1)
        ring_send(2)
        await_bytes(tfull.at[pl.ds(0, NY - 1)], rsem.at[8])
        for j in range(NY):
            tbuf[:, j * NM:(j + 1) * NM] = tfull[j, :, :NM]
        tbuf[:, NY * NM:] = jnp.sum(tfull[:, :, NM:], axis=0)
        for i, p in enumerate(sect_peers):
            send(tbuf, tbuf, 16 + i, p, rsem.at[9])
        ring_wait(2)
        ring_send(3)
        ring_wait(3)
        ring_send(4)
        await_bytes(dyr, rsem.at[11])
        await_bytes(irecv.at[pl.ds(0, NS - 1)], ssem.at[6])
        await_bytes(tfull.at[pl.ds(0, NY - 1)], ssem.at[8])
        for i in range(NS - 1):
            await_bytes(tbuf, ssem.at[16 + i])

    @pl.when(jnp.logical_not(is_txt))
    def _():
        irecv[s] = psend[s - 1]
        await_bytes(irecv.at[pl.ds(0, NS - 1)], rsem.at[6])
        ifull[y] = jnp.sum(irecv[...], axis=0)
        for p in y_peers:
            send(ifull.at[y], ifull.at[y], 8, p)
        ring_wait(1)
        ring_send(2)
        await_bytes(ifull.at[pl.ds(0, NY - 1)], rsem.at[8])
        fv = ifull[...]
        extra = jnp.sum(fv[:, :, NM:], axis=0)
        unit, _ = unit_rows(jnp.concatenate([fv[j, :, :NM] for j in range(NY)] + [extra], axis=1))
        emb[zx] = unit.astype(BF)
        for p in zx_peers:
            send(emb.at[zx], emb.at[zx], 9, p, rsem.at[10])
        ring_wait(2)
        ring_send(3)
        NI = NZX * 8
        at_img = pos[0:NI]
        for j in range(1, NS - 1):
            at_img = jnp.where(s == j + 1, pos[j * NI:(j + 1) * NI], at_img)
        hit = at_img[None] == NT * blk + iota((4, NI), 0)
        label = jnp.where(hit, 1.0, -1.0)
        await_bytes(tbuf, rsem.at[9])
        t_unit, t_inv = unit_rows(tbuf[...])
        t_emb = t_unit.astype(BF)
        ring_wait(3)
        ring_send(4)
        await_bytes(emb.at[pl.ds(0, NZX - 1)], rsem.at[10])
        ev = emb[...].reshape(NI, NY * NM + NE)
        logits = m_ * dot_nt(t_emb, ev) + off[0]
        coef = -label * jax.nn.sigmoid(-label * logits)
        coef = jnp.where(iota(coef.shape, 0) < NT, coef, 0.0).astype(BF)
        g = m_ * dot_nn(coef, ev)
        gp = (g - t_unit * jnp.sum(t_unit * g, axis=-1, keepdims=True)) * t_inv
        slot = x * (NS - 1) + s - 1
        dyr[slot] = gp.astype(DY)
        for dx in x_far + [0]:
            for ds in range(NS):
                if dx or ds:
                    peer = {"sect": lax.rem(s + ds, NS), "blk_1": lax.rem(x + dx, NX)}
                    send(dyr.at[slot], dyr.at[slot], 13, peer, rsem.at[11])
        await_bytes(dyr.at[pl.ds(0, n_dy - 1)], rsem.at[11])
        await_bytes(ifull.at[pl.ds(0, NY - 1)], ssem.at[8])
        await_bytes(emb.at[pl.ds(0, NZX - 1)], ssem.at[9])
        await_bytes(emit.at[pl.ds(0, NX * NS - 1)], ssem.at[13])
        await_bytes(irecv.at[pl.ds(0, NS - 2)], ssem.at[6])
        await_bytes(ptx, ssem.at[7])

    for j in range(NX):
        v = sum(dyr[(NS - 1) * j + i].astype(F32) for i in range(NS - 1))
        dls[4 * j:4 * j + 4, :] = v
    n_m, per_y = NY * NZ * K8, NZ * K8
    lane = iota((NX * 4, NM), 1)
    halves = []
    for h in range(n_m // NM):
        t = jnp.zeros((NX * 4, NM), F32)
        for i in range(NM // per_y):
            v = dls[:, (h * (NM // per_y) + i) * NM:(h * (NM // per_y) + i + 1) * NM]
            v = pltpu.roll(v, lax.rem(i * per_y - x * per_y + NM, NM), 1)
            t = jnp.where(lax.div(lane, per_y) == i, v, t)
        halves.append(t)
    d_m = jnp.concatenate(halves, axis=1).astype(BF)
    v = dls[:, NY * NM:]
    t = jnp.zeros((NX * 4, NE), F32)
    for j in range(NY):
        r = pltpu.roll(v, lax.rem(j * NZ - j * NZX - x * NZ + 2 * NE, NE), 1)
        t = jnp.where(lax.div(lane, NZ) == j, r, t)
    d_e = t[:, :NY * NZ].astype(BF)
    ring_wait(4)
    for j in range(NY):
        wes[NZ * j:NZ * (j + 1), :] = we[j]
    o = dot_nn(d_m, wf[...].reshape(n_m, LP)) + dot_nn(d_e, wes[...].astype(BF))
    for j in range(NX):
        osend[j] = o[4 * j:4 * j + 4].astype(OT)
    orecv[x] = osend[x]
    for d, p in zip(x_far, x_peers):
        send(osend.at[lax.rem(x + d, NX)], orecv.at[x], 12, p)
    await_bytes(orecv.at[pl.ds(0, NX - 1)], rsem.at[12])
    out[...] = jnp.sum(orecv[...].astype(F32), axis=0)[:NT, :FFQ]

    await_bytes(hrecv.at[pl.ds(0, NS - 1)], ssem.at[0])
    for k, ref in ((1, wm), (2, wx)):
        n_z = 2 * (NZ - 1)
        await_bytes(ref.at[0, pl.ds(0, n_z)], ssem.at[k])
    for k, ref in ((3, wm), (4, wx), (19, wm), (20, wx)):
        await_bytes(ref.at[0, pl.ds(0, nx_in)], ssem.at[k])
    for k, far in ((0, NY // 2), (1, NY - 1 - NY // 2)):
        await_bytes(wf.at[pl.ds(0, far)], ssem.at[10 + k])
        await_bytes(we.at[pl.ds(0, far)], ssem.at[14 + k])
    await_bytes(hall.at[pl.ds(0, NY - 1)], ssem.at[5])
    await_bytes(orecv.at[pl.ds(0, NX - 1)], ssem.at[12])


def on_device(hidden, w_txt, w_img, b_txt, b_img, mult, off, pos):
    NS, NZ, NX, NY = (lax.axis_size(a) for a in SECT_BLK)
    _, rows, FF = hidden.shape
    D = b_txt.shape[0]
    K = w_txt.shape[1]
    NZX = NZ * NX
    NM, NE = NZX * K8, NZX * NY
    FFQ = FF // NS
    LP = (FFQ + 3 + 127) // 128 * 128
    dims = (NS, NZ, NX, NY, FF)
    vm = pltpu.VMEM
    scratch = [
        vm((rows, FF), BF),
        vm((2, K, FF), BF),
        vm((K, LP), F32),
        vm((2, NZX, K8, LP), BF),
        vm((2, NZX, 1, LP), F32),
        vm((2, NZX, LP), F32),
        vm((NS, 4, LP), BF),
        vm((NS, 4, LP), BF),
        vm((NY, 8, LP), BF),
        vm((2, NE, LP), BF),
        vm((2 * NY * 8 + 8, NM), F32),
        vm((NT, NY, NM + NE), F32),
        vm((NY, 4, NM + NE), F32),
        vm((NS, NY, NM + NE), F32),
        vm((NS, NY, 4, NM + NE), F32),
        vm((NY, NY, NM + NE), F32),
        vm((NY, 4, NM + NE), F32),
        vm((NY, 4, NM + NE), F32),
        vm((4, D), F32),
        vm((NZX, 8, D), BF),
        vm((NX * NS, 4, D), DY),
        vm((NX * (NS - 1), 4, D), DY),
        vm((NX * 4, D), F32),
        vm((NX, 4, LP), OT),
        vm((NX, 4, LP), OT),
        vm((NY, NZ * K8, LP), BF),
        vm((NY, NZ, LP), F32),
        vm((NY * NZ, LP), F32),
        vm((D,), F32),
        vm((D,), F32),
        vm(pos.shape, jnp.int32),
        pltpu.SemaphoreType.DMA((6,)),
        pltpu.SemaphoreType.DMA((21,)),
        pltpu.SemaphoreType.DMA((13,)),
        pltpu.SemaphoreType.DMA((2, NZ - 1, 2)),
        pltpu.SemaphoreType.DMA((2, 2)),
        pltpu.SemaphoreType.DMA((2, NY // 2, 2)),
    ]
    any_ = pl.BlockSpec(memory_space=pl.ANY)
    vmem = pl.BlockSpec(memory_space=pltpu.VMEM)
    smem = pl.BlockSpec(memory_space=pltpu.SMEM)
    return pl.pallas_call(
        functools.partial(kernel, dims),
        out_shape=pltpu.VMEM((NT, FFQ), F32),
        in_specs=[any_, any_, any_, any_, any_, smem, smem, any_],
        out_specs=vmem,
        scratch_shapes=scratch,
        compiler_params=pltpu.CompilerParams(collective_id=0, has_side_effects=True),
    )(
        hidden[0], w_txt.T, w_img.T, b_txt, b_img, mult, off, pos
    )


def solution(mesh):
    finer = Mesh(
        mesh.devices.reshape(mesh.shape["sect"], 4, 4, 8), ("sect", "blk_0", "blk_1", "blk_2")
    )
    placed = (P(SECT_BLK, None, None), P(None, BLK), P(None, BLK), P(), P(), P(), P(), P())
    return jax.shard_map(
        on_device, mesh=finer, in_specs=placed, out_specs=P(BLK, "sect"), check_vma=False
    )
```

```python
import functools

import jax
import jax.numpy as jnp
from jax import lax
from jax.experimental import pallas as pl
from jax.experimental.pallas import tpu as pltpu
from jax.sharding import Mesh
from jax.sharding import PartitionSpec as P

TXT_LEN = 64
NT = 3
K8 = 8
BF = jnp.bfloat16
F32 = jnp.float32
BLK = ("blk_0", "blk_1", "blk_2")
SECT_BLK = ("sect", "blk_0", "blk_1", "blk_2")
MESH = pl.DeviceIdType.MESH
DY = F32
OT = F32


def iota(shape, dim):
    return lax.broadcasted_iota(jnp.int32, shape, dim)


def dot_nn(a, b):
    return lax.dot_general(a, b, (((1,), (0,)), ((), ())), preferred_element_type=F32)


def dot_nt(a, b):
    return lax.dot_general(a, b, (((1,), (1,)), ((), ())), preferred_element_type=F32)


def unit_rows(p):
    inv = lax.rsqrt(jnp.sum(p * p, axis=-1, keepdims=True) + 1e-06)
    return p * inv, inv


def kernel(
    dims,
    hid, wt, wi, bt_hbm, bi_hbm, mult, off, pos_hbm,
    out,
    hv, wv, wtmp, wm, wx, xpad,
    hsend, hrecv, hall,
    xe, pscr, psend, ptx, irecv, trecv, ifull, tsum, tfull,
    tbuf, emb, emit, dyr, dls, osend, orecv,
    wf, we, wes,
    bt, bi, pos, lsem, ssem, rsem, zsem, xsem, ysem,
):
    NS, NZ, NX, NY, FF = dims
    FFQ = FF // NS
    LP = wtmp.shape[1]
    NZX = NZ * NX
    NM = NZX * K8
    NE = NZX * NY
    s = lax.axis_index("sect")
    z = lax.axis_index("blk_0")
    x = lax.axis_index("blk_1")
    y = lax.axis_index("blk_2")
    zx = z * NX + x
    blk = zx * NY + y

    sect_peers = [{"sect": lax.rem(s + d, NS)} for d in range(1, NS)]
    y_far = sorted(range(1, NY), key=lambda d: -min(d, NY - d))
    y_peers = [{"blk_2": lax.rem(y + d, NY)} for d in y_far]
    z_peers = [{"blk_0": lax.rem(z + d, NZ)} for d in range(1, NZ)]
    x_far = sorted(range(1, NX), key=lambda d: -min(d, NX - d))
    x_peers = [{"blk_1": lax.rem(x + d, NX)} for d in x_far]
    zx_peers = []
    far = [(dz, dx) for dz in range(NZ) for dx in range(NX)][1:]
    far = sorted(far, key=lambda d: -2 * min(d[0], NZ - d[0]) - min(d[1], NX - d[1]))
    for dz, dx in far:
        zx_peers.append({"blk_0": lax.rem(z + dz, NZ), "blk_1": lax.rem(x + dx, NX)})

    loads = [
        pltpu.make_async_copy(wi, wv.at[0], lsem.at[0]),
        pltpu.make_async_copy(wt, wv.at[1], lsem.at[1]),
        pltpu.make_async_copy(hid, hv, lsem.at[2]),
        pltpu.make_async_copy(bi_hbm, bi, lsem.at[3]),
        pltpu.make_async_copy(bt_hbm, bt, lsem.at[4]),
        pltpu.make_async_copy(pos_hbm, pos, lsem.at[5]),
    ]
    for c in loads:
        c.start()
    barrier = pltpu.get_barrier_semaphore()
    everyone = sect_peers + y_peers + x_peers + z_peers
    for p in everyone:
        pl.semaphore_signal(barrier, inc=1, device_id=p, device_id_type=MESH)

    def send(src, dst, k, peer, recv=None):
        pltpu.make_async_remote_copy(
            src_ref=src, dst_ref=dst, send_sem=ssem.at[k],
            recv_sem=rsem.at[k] if recv is None else recv,
            device_id=peer, device_id_type=MESH,
        ).start()

    def await_bytes(ref, sem):
        pltpu.make_async_copy(ref, ref, sem).wait()

    me = x * NZ + z
    for m, b in ((0, bi), (1, bt)):
        loads[m].wait()
        loads[3 + m].wait()
        w32 = wv[m].astype(F32)
        wtmp[...] = jnp.zeros_like(wtmp)
        for q in range(NS):
            @pl.when(s == q)
            def _(q=q, w32=w32):
                wtmp[:, :FFQ] = w32[:, q * FFQ:(q + 1) * FFQ]
        v = wtmp[...]
        brow = jnp.broadcast_to(b[...][None], (K8 + 1, b.shape[0]))
        pick = iota(brow.shape, 1) == blk * (K8 + 1) + iota(brow.shape, 0)
        bcol = jnp.sum(jnp.where(pick, brow, 0.0), axis=1, keepdims=True)
        hi = bcol.astype(BF).astype(F32)
        lo = (bcol - hi).astype(BF).astype(F32)
        lane = iota(v.shape, 1)
        v = jnp.where(lane == FFQ, hi, v)
        v = jnp.where(lane == FFQ + 1, lo, v)
        v = jnp.where(lane == FFQ + 2, bcol - hi - lo, v)
        wm[m, me] = v[:K8].astype(BF)
        wx[m, me] = v[K8:].astype(BF).astype(F32)

    rows = hv.shape[0]
    r8 = iota((8, rows), 0)
    t8 = iota((8, rows), 1)
    is_txt = s == 0
    at = (lax.shift_right_logical(t8, 6) == r8).astype(F32)
    ai = (r8 == s - 1).astype(F32)
    f_txt = is_txt.astype(F32)
    a = (f_txt * at + (1.0 - f_txt) * ai).astype(BF)
    scale = jnp.where(is_txt, 1.0 / TXT_LEN, 1.0 / rows)
    loads[2].wait()
    loads[5].wait()
    hsum = dot_nn(a, hv[...]) * scale
    hsend[...] = jnp.zeros_like(hsend)
    for q in range(NS):
        hsend[q, :, :FFQ] = hsum[:4, q * FFQ:(q + 1) * FFQ].astype(BF)
    hrecv[s] = hsend[s]
    xe[...] = jnp.zeros_like(xe)
    dls[...] = jnp.zeros_like(dls)

    pl.semaphore_wait(barrier, len(everyone))

    for d in range(1, NS):
        send(hsend.at[lax.rem(s + d, NS)], hrecv.at[s], 0, sect_peers[d - 1])
    def own_z(m):
        for i in range(NZ - 1):
            send(wm.at[m, me], wm.at[m, me], 1, z_peers[i], zsem.at[m, i, 0])
            send(wx.at[m, me], wx.at[m, me], 2, z_peers[i], zsem.at[m, i, 1])

    def own_x(m):
        for p in x_peers:
            send(wm.at[m, me], wm.at[m, me], 3 + 16 * m, p, xsem.at[m, 0])

    own_z(0)
    own_x(0)
    own_x(1)
    await_bytes(hrecv.at[pl.ds(0, NS - 1)], rsem.at[0])
    hr = hrecv[...].astype(F32)
    hq = jnp.concatenate([hr[0], hr[1] + hr[2] + hr[3]], axis=0)
    lane = iota(hq.shape, 1)
    ones = ((lane >= FFQ) & (lane < FFQ + 3)).astype(F32) * f_txt
    hall[y] = (hq + ones).astype(BF)
    for p in y_peers:
        send(hall.at[y], hall.at[y], 5, p)
    own_z(1)
    for m in range(2):
        for i in sorted(range(NZ - 1), key=lambda i: min(i + 1, NZ - 1 - i)):
            sl = x * NZ + lax.rem(z + NZ - (i + 1), NZ)
            await_bytes(wm.at[m, sl], zsem.at[m, i, 0])
            for p in x_peers:
                send(wm.at[m, sl], wm.at[m, sl], 3 + 16 * m, p, xsem.at[m, 0])
        for i in range(NZ - 1):
            sl = x * NZ + lax.rem(z + NZ - (i + 1), NZ)
            await_bytes(wx.at[m, sl], zsem.at[m, i, 1])
        four = wx.at[m, pl.ds(x * NZ, NZ)]
        for p in x_peers:
            send(four, four, 4 + 16 * m, p, xsem.at[m, 1])
    await_bytes(hall.at[pl.ds(0, NY - 1)], rsem.at[5])
    hrows = hall[...].reshape(NY * 8, LP)
    nx_in = (NX - 1) * NZ

    wf[y] = wm[1, pl.ds(x * NZ, NZ)].reshape(NZ * K8, LP)
    for j in range(NZ):
        we[y, j:j + 1, :] = wx[1, x * NZ + j]

    def ring_send(t):
        for k, far, hop in ((0, NY // 2, 1), (1, NY - 1 - NY // 2, NY - 1)):
            if t <= far:
                c = lax.rem(y + (NY - hop) * (t - 1), NY)
                p = {"blk_2": lax.rem(y + hop, NY)}
                send(wf.at[c], wf.at[c], 10 + k, p, ysem.at[k, t - 1, 0])
                send(we.at[c], we.at[c], 14 + k, p, ysem.at[k, t - 1, 1])

    def ring_wait(t):
        for k, far, hop in ((0, NY // 2, 1), (1, NY - 1 - NY // 2, NY - 1)):
            if t <= far:
                c = lax.rem(y + (NY - hop) * t, NY)
                await_bytes(wf.at[c], ysem.at[k, t - 1, 0])
                await_bytes(we.at[c], ysem.at[k, t - 1, 1])

    ring_send(1)

    def tile(m):
        await_bytes(wm.at[m, pl.ds(0, nx_in)], xsem.at[m, 0])
        pm = dot_nt(hrows, wm[m].reshape(NM, LP))
        await_bytes(wx.at[m, pl.ds(0, nx_in)], xsem.at[m, 1])
        for j in range(NZX):
            xpad[m, j:j + 1, :] = wx[m, j]
        xe[m, pl.ds(pl.multiple_of(y * NZX, NZX), NZX), :] = xpad[m].astype(BF)
        pe = dot_nt(hrows, xe[m])
        if m:
            for j in range(NY):
                ptx[j, :, :NM] = pm[8 * j:8 * j + 4]
                ptx[j, :, NM:] = pe[8 * j:8 * j + 4]
        else:
            pscr[:NY * 8] = pm
            pscr[NY * 8:2 * NY * 8] = pe
            for r in range(NT):
                psend[r, :, :NM] = pscr[pl.ds(4 + r, NY, stride=8), :]
                psend[r, :, NM:] = pscr[pl.ds(NY * 8 + 4 + r, NY, stride=8), :]

    tile(0)
    for d in range(1, NS):
        sp = lax.rem(s + d, NS)

        @pl.when(sp != 0)
        def _(d=d, sp=sp):
            send(psend.at[sp - 1], irecv.at[s], 6, sect_peers[d - 1])
    tile(1)
    for d in range(1, NS):
        sp = lax.rem(s + d, NS)

        @pl.when(sp == 0)
        def _(d=d):
            send(ptx, trecv.at[s], 7, sect_peers[d - 1])

    m_ = mult[0]
    n_dy = NX * (NS - 1)

    @pl.when(is_txt)
    def _():
        trecv[0] = ptx[...]
        await_bytes(trecv.at[pl.ds(0, NS - 1)], rsem.at[7])
        tsum[...] = jnp.sum(trecv[...], axis=0)
        tfull[y] = tsum[y]
        for d, p in zip(y_far, y_peers):
            send(tsum.at[lax.rem(y + d, NY)], tfull.at[y], 8, p)
        ring_wait(1)
        ring_send(2)
        await_bytes(tfull.at[pl.ds(0, NY - 1)], rsem.at[8])
        for j in range(NY):
            tbuf[:, j * NM:(j + 1) * NM] = tfull[j, :, :NM]
        tbuf[:, NY * NM:] = jnp.sum(tfull[:, :, NM:], axis=0)
        for i, p in enumerate(sect_peers):
            send(tbuf, tbuf, 16 + i, p, rsem.at[9])
        ring_wait(2)
        ring_send(3)
        ring_wait(3)
        ring_send(4)
        await_bytes(dyr, rsem.at[11])
        await_bytes(irecv.at[pl.ds(0, NS - 1)], ssem.at[6])
        await_bytes(tfull.at[pl.ds(0, NY - 1)], ssem.at[8])
        for i in range(NS - 1):
            await_bytes(tbuf, ssem.at[16 + i])

    @pl.when(jnp.logical_not(is_txt))
    def _():
        irecv[s] = psend[s - 1]
        await_bytes(irecv.at[pl.ds(0, NS - 1)], rsem.at[6])
        ifull[y] = jnp.sum(irecv[...], axis=0)
        for p in y_peers:
            send(ifull.at[y], ifull.at[y], 8, p)
        ring_wait(1)
        ring_send(2)
        await_bytes(ifull.at[pl.ds(0, NY - 1)], rsem.at[8])
        fv = ifull[...]
        extra = jnp.sum(fv[:, :, NM:], axis=0)
        unit, _ = unit_rows(jnp.concatenate([fv[j, :, :NM] for j in range(NY)] + [extra], axis=1))
        emb[zx] = unit.astype(BF)
        for p in zx_peers:
            send(emb.at[zx], emb.at[zx], 9, p, rsem.at[10])
        ring_wait(2)
        ring_send(3)
        NI = NZX * 8
        at_img = pos[0:NI]
        for j in range(1, NS - 1):
            at_img = jnp.where(s == j + 1, pos[j * NI:(j + 1) * NI], at_img)
        hit = at_img[None] == NT * blk + iota((4, NI), 0)
        label = jnp.where(hit, 1.0, -1.0)
        await_bytes(tbuf, rsem.at[9])
        t_unit, t_inv = unit_rows(tbuf[...])
        t_emb = t_unit.astype(BF)
        ring_wait(3)
        ring_send(4)
        await_bytes(emb.at[pl.ds(0, NZX - 1)], rsem.at[10])
        ev = emb[...].reshape(NI, NY * NM + NE)
        logits = m_ * dot_nt(t_emb, ev) + off[0]
        coef = -label * jax.nn.sigmoid(-label * logits)
        coef = jnp.where(iota(coef.shape, 0) < NT, coef, 0.0).astype(BF)
        g = m_ * dot_nn(coef, ev)
        gp = (g - t_unit * jnp.sum(t_unit * g, axis=-1, keepdims=True)) * t_inv
        slot = x * (NS - 1) + s - 1
        dyr[slot] = gp.astype(DY)
        for dx in x_far + [0]:
            for ds in range(NS):
                if dx or ds:
                    peer = {"sect": lax.rem(s + ds, NS), "blk_1": lax.rem(x + dx, NX)}
                    send(dyr.at[slot], dyr.at[slot], 13, peer, rsem.at[11])
        await_bytes(dyr.at[pl.ds(0, n_dy - 1)], rsem.at[11])
        await_bytes(ifull.at[pl.ds(0, NY - 1)], ssem.at[8])
        await_bytes(emb.at[pl.ds(0, NZX - 1)], ssem.at[9])
        await_bytes(emit.at[pl.ds(0, NX * NS - 1)], ssem.at[13])
        await_bytes(irecv.at[pl.ds(0, NS - 2)], ssem.at[6])
        await_bytes(ptx, ssem.at[7])

    for j in range(NX):
        v = sum(dyr[(NS - 1) * j + i].astype(F32) for i in range(NS - 1))
        dls[4 * j:4 * j + 4, :] = v
    n_m, per_y = NY * NZ * K8, NZ * K8
    lane = iota((NX * 4, NM), 1)
    halves = []
    for h in range(n_m // NM):
        t = jnp.zeros((NX * 4, NM), F32)
        for i in range(NM // per_y):
            v = dls[:, (h * (NM // per_y) + i) * NM:(h * (NM // per_y) + i + 1) * NM]
            v = pltpu.roll(v, lax.rem(i * per_y - x * per_y + NM, NM), 1)
            t = jnp.where(lax.div(lane, per_y) == i, v, t)
        halves.append(t)
    d_m = jnp.concatenate(halves, axis=1).astype(BF)
    v = dls[:, NY * NM:]
    t = jnp.zeros((NX * 4, NE), F32)
    for j in range(NY):
        r = pltpu.roll(v, lax.rem(j * NZ - j * NZX - x * NZ + 2 * NE, NE), 1)
        t = jnp.where(lax.div(lane, NZ) == j, r, t)
    d_e = t[:, :NY * NZ].astype(BF)
    ring_wait(4)
    for j in range(NY):
        wes[NZ * j:NZ * (j + 1), :] = we[j]
    o = dot_nn(d_m, wf[...].reshape(n_m, LP)) + dot_nn(d_e, wes[...].astype(BF))
    for j in range(NX):
        osend[j] = o[4 * j:4 * j + 4].astype(OT)
    orecv[x] = osend[x]
    for d, p in zip(x_far, x_peers):
        send(osend.at[lax.rem(x + d, NX)], orecv.at[x], 12, p)
    await_bytes(orecv.at[pl.ds(0, NX - 1)], rsem.at[12])
    out[...] = jnp.sum(orecv[...].astype(F32), axis=0)[:NT, :FFQ]

    await_bytes(hrecv.at[pl.ds(0, NS - 1)], ssem.at[0])
    for k, ref in ((1, wm), (2, wx)):
        n_z = 2 * (NZ - 1)
        await_bytes(ref.at[0, pl.ds(0, n_z)], ssem.at[k])
    for k, ref in ((3, wm), (4, wx), (19, wm), (20, wx)):
        await_bytes(ref.at[0, pl.ds(0, nx_in)], ssem.at[k])
    for k, far in ((0, NY // 2), (1, NY - 1 - NY // 2)):
        await_bytes(wf.at[pl.ds(0, far)], ssem.at[10 + k])
        await_bytes(we.at[pl.ds(0, far)], ssem.at[14 + k])
    await_bytes(hall.at[pl.ds(0, NY - 1)], ssem.at[5])
    await_bytes(orecv.at[pl.ds(0, NX - 1)], ssem.at[12])


def on_device(hidden, w_txt, w_img, b_txt, b_img, mult, off, pos):
    NS, NZ, NX, NY = (lax.axis_size(a) for a in SECT_BLK)
    _, rows, FF = hidden.shape
    D = b_txt.shape[0]
    K = w_txt.shape[1]
    NZX = NZ * NX
    NM, NE = NZX * K8, NZX * NY
    FFQ = FF // NS
    LP = (FFQ + 3 + 127) // 128 * 128
    dims = (NS, NZ, NX, NY, FF)
    vm = pltpu.VMEM
    scratch = [
        vm((rows, FF), BF),
        vm((2, K, FF), BF),
        vm((K, LP), F32),
        vm((2, NZX, K8, LP), BF),
        vm((2, NZX, 1, LP), F32),
        vm((2, NZX, LP), F32),
        vm((NS, 4, LP), BF),
        vm((NS, 4, LP), BF),
        vm((NY, 8, LP), BF),
        vm((2, NE, LP), BF),
        vm((2 * NY * 8 + 8, NM), F32),
        vm((NT, NY, NM + NE), F32),
        vm((NY, 4, NM + NE), F32),
        vm((NS, NY, NM + NE), F32),
        vm((NS, NY, 4, NM + NE), F32),
        vm((NY, NY, NM + NE), F32),
        vm((NY, 4, NM + NE), F32),
        vm((NY, 4, NM + NE), F32),
        vm((4, D), F32),
        vm((NZX, 8, D), BF),
        vm((NX * NS, 4, D), DY),
        vm((NX * (NS - 1), 4, D), DY),
        vm((NX * 4, D), F32),
        vm((NX, 4, LP), OT),
        vm((NX, 4, LP), OT),
        vm((NY, NZ * K8, LP), BF),
        vm((NY, NZ, LP), F32),
        vm((NY * NZ, LP), F32),
        vm((D,), F32),
        vm((D,), F32),
        vm(pos.shape, jnp.int32),
        pltpu.SemaphoreType.DMA((6,)),
        pltpu.SemaphoreType.DMA((21,)),
        pltpu.SemaphoreType.DMA((13,)),
        pltpu.SemaphoreType.DMA((2, NZ - 1, 2)),
        pltpu.SemaphoreType.DMA((2, 2)),
        pltpu.SemaphoreType.DMA((2, NY // 2, 2)),
    ]
    any_ = pl.BlockSpec(memory_space=pl.ANY)
    vmem = pl.BlockSpec(memory_space=pltpu.VMEM)
    smem = pl.BlockSpec(memory_space=pltpu.SMEM)
    return pl.pallas_call(
        functools.partial(kernel, dims),
        out_shape=pltpu.VMEM((NT, FFQ), F32),
        in_specs=[any_, any_, any_, any_, any_, smem, smem, any_],
        out_specs=vmem,
        scratch_shapes=scratch,
        compiler_params=pltpu.CompilerParams(collective_id=0, has_side_effects=True),
    )(
        hidden[0], w_txt.T, w_img.T, b_txt, b_img, mult, off, pos
    )


def solution(mesh):
    finer = Mesh(
        mesh.devices.reshape(mesh.shape["sect"], 4, 4, 8), ("sect", "blk_0", "blk_1", "blk_2")
    )
    placed = (P(SECT_BLK, None, None), P(None, BLK), P(None, BLK), P(), P(), P(), P(), P())
    return jax.shard_map(
        on_device, mesh=finer, in_specs=placed, out_specs=P(BLK, "sect"), check_vma=False
    )
```

```python
import functools

import jax
import jax.numpy as jnp
from jax import lax
from jax.experimental import pallas as pl
from jax.experimental.pallas import tpu as pltpu
from jax.sharding import Mesh
from jax.sharding import PartitionSpec as P

TXT_LEN = 64
NT = 3
K8 = 8
BF = jnp.bfloat16
F32 = jnp.float32
BLK = ("blk_0", "blk_1", "blk_2")
SECT_BLK = ("sect", "blk_0", "blk_1", "blk_2")
MESH = pl.DeviceIdType.MESH
DY = F32
OT = F32


def iota(shape, dim):
    return lax.broadcasted_iota(jnp.int32, shape, dim)


def dot_nn(a, b):
    return lax.dot_general(a, b, (((1,), (0,)), ((), ())), preferred_element_type=F32)


def dot_nt(a, b):
    return lax.dot_general(a, b, (((1,), (1,)), ((), ())), preferred_element_type=F32)


def unit_rows(p):
    inv = lax.rsqrt(jnp.sum(p * p, axis=-1, keepdims=True) + 1e-06)
    return p * inv, inv


def kernel(
    dims,
    hid, wt, wi, bt_hbm, bi_hbm, mult, off, pos_hbm,
    out,
    hv, wv, wtmp, wm, wx, xpad,
    hsend, hrecv, hall,
    xe, pscr, psend, ptx, irecv, trecv, ifull, tsum, tfull,
    tbuf, emb, emit, dyr, dls, osend, orecv,
    wf, we, wes,
    bt, bi, pos, lsem, ssem, rsem, zsem, xsem, ysem,
):
    NS, NZ, NX, NY, FF = dims
    FFQ = FF // NS
    LP = wtmp.shape[1]
    NZX = NZ * NX
    NM = NZX * K8
    NE = NZX * NY
    s = lax.axis_index("sect")
    z = lax.axis_index("blk_0")
    x = lax.axis_index("blk_1")
    y = lax.axis_index("blk_2")
    zx = z * NX + x
    blk = zx * NY + y

    sect_peers = [{"sect": lax.rem(s + d, NS)} for d in range(1, NS)]
    y_far = sorted(range(1, NY), key=lambda d: -min(d, NY - d))
    y_peers = [{"blk_2": lax.rem(y + d, NY)} for d in y_far]
    z_peers = [{"blk_0": lax.rem(z + d, NZ)} for d in range(1, NZ)]
    x_far = sorted(range(1, NX), key=lambda d: -min(d, NX - d))
    x_peers = [{"blk_1": lax.rem(x + d, NX)} for d in x_far]
    zx_peers = []
    far = [(dz, dx) for dz in range(NZ) for dx in range(NX)][1:]
    far = sorted(far, key=lambda d: -2 * min(d[0], NZ - d[0]) - min(d[1], NX - d[1]))
    for dz, dx in far:
        zx_peers.append({"blk_0": lax.rem(z + dz, NZ), "blk_1": lax.rem(x + dx, NX)})

    loads = [
        pltpu.make_async_copy(wi, wv.at[0], lsem.at[0]),
        pltpu.make_async_copy(wt, wv.at[1], lsem.at[1]),
        pltpu.make_async_copy(hid, hv, lsem.at[2]),
        pltpu.make_async_copy(bi_hbm, bi, lsem.at[3]),
        pltpu.make_async_copy(bt_hbm, bt, lsem.at[4]),
        pltpu.make_async_copy(pos_hbm, pos, lsem.at[5]),
    ]
    for c in loads:
        c.start()
    barrier = pltpu.get_barrier_semaphore()
    everyone = sect_peers + y_peers + x_peers + z_peers
    for p in everyone:
        pl.semaphore_signal(barrier, inc=1, device_id=p, device_id_type=MESH)

    def send(src, dst, k, peer, recv=None):
        pltpu.make_async_remote_copy(
            src_ref=src, dst_ref=dst, send_sem=ssem.at[k],
            recv_sem=rsem.at[k] if recv is None else recv,
            device_id=peer, device_id_type=MESH,
        ).start()

    def await_bytes(ref, sem):
        pltpu.make_async_copy(ref, ref, sem).wait()

    me = x * NZ + z
    for m, b in ((0, bi), (1, bt)):
        loads[m].wait()
        loads[3 + m].wait()
        w32 = wv[m].astype(F32)
        wtmp[...] = jnp.zeros_like(wtmp)
        for q in range(NS):
            @pl.when(s == q)
            def _(q=q, w32=w32):
                wtmp[:, :FFQ] = w32[:, q * FFQ:(q + 1) * FFQ]
        v = wtmp[...]
        brow = jnp.broadcast_to(b[...][None], (K8 + 1, b.shape[0]))
        pick = iota(brow.shape, 1) == blk * (K8 + 1) + iota(brow.shape, 0)
        bcol = jnp.sum(jnp.where(pick, brow, 0.0), axis=1, keepdims=True)
        hi = bcol.astype(BF).astype(F32)
        lo = (bcol - hi).astype(BF).astype(F32)
        lane = iota(v.shape, 1)
        v = jnp.where(lane == FFQ, hi, v)
        v = jnp.where(lane == FFQ + 1, lo, v)
        v = jnp.where(lane == FFQ + 2, bcol - hi - lo, v)
        wm[m, me] = v[:K8].astype(BF)
        wx[m, me] = v[K8:].astype(BF).astype(F32)

    rows = hv.shape[0]
    r8 = iota((8, rows), 0)
    t8 = iota((8, rows), 1)
    is_txt = s == 0
    at = (lax.shift_right_logical(t8, 6) == r8).astype(F32)
    ai = (r8 == s - 1).astype(F32)
    f_txt = is_txt.astype(F32)
    a = (f_txt * at + (1.0 - f_txt) * ai).astype(BF)
    scale = jnp.where(is_txt, 1.0 / TXT_LEN, 1.0 / rows)
    loads[2].wait()
    loads[5].wait()
    hsum = dot_nn(a, hv[...]) * scale
    hsend[...] = jnp.zeros_like(hsend)
    for q in range(NS):
        hsend[q, :, :FFQ] = hsum[:4, q * FFQ:(q + 1) * FFQ].astype(BF)
    hrecv[s] = hsend[s]
    xe[...] = jnp.zeros_like(xe)
    dls[...] = jnp.zeros_like(dls)

    pl.semaphore_wait(barrier, len(everyone))

    for d in range(1, NS):
        send(hsend.at[lax.rem(s + d, NS)], hrecv.at[s], 0, sect_peers[d - 1])
    def own_z(m):
        for i in range(NZ - 1):
            send(wm.at[m, me], wm.at[m, me], 1, z_peers[i], zsem.at[m, i, 0])
            send(wx.at[m, me], wx.at[m, me], 2, z_peers[i], zsem.at[m, i, 1])

    def own_x(m):
        for p in x_peers:
            send(wm.at[m, me], wm.at[m, me], 3 + 16 * m, p, xsem.at[m, 0])

    own_z(0)
    own_x(0)
    own_x(1)
    await_bytes(hrecv.at[pl.ds(0, NS - 1)], rsem.at[0])
    hr = hrecv[...].astype(F32)
    hq = jnp.concatenate([hr[0], hr[1] + hr[2] + hr[3]], axis=0)
    lane = iota(hq.shape, 1)
    ones = ((lane >= FFQ) & (lane < FFQ + 3)).astype(F32) * f_txt
    hall[y] = (hq + ones).astype(BF)
    for p in y_peers:
        send(hall.at[y], hall.at[y], 5, p)
    own_z(1)
    for m in range(2):
        for i in sorted(range(NZ - 1), key=lambda i: min(i + 1, NZ - 1 - i)):
            sl = x * NZ + lax.rem(z + NZ - (i + 1), NZ)
            await_bytes(wm.at[m, sl], zsem.at[m, i, 0])
            for p in x_peers:
                send(wm.at[m, sl], wm.at[m, sl], 3 + 16 * m, p, xsem.at[m, 0])
        for i in range(NZ - 1):
            sl = x * NZ + lax.rem(z + NZ - (i + 1), NZ)
            await_bytes(wx.at[m, sl], zsem.at[m, i, 1])
        four = wx.at[m, pl.ds(x * NZ, NZ)]
        for p in x_peers:
            send(four, four, 4 + 16 * m, p, xsem.at[m, 1])
    await_bytes(hall.at[pl.ds(0, NY - 1)], rsem.at[5])
    hrows = hall[...].reshape(NY * 8, LP)
    nx_in = (NX - 1) * NZ

    wf[y] = wm[1, pl.ds(x * NZ, NZ)].reshape(NZ * K8, LP)
    for j in range(NZ):
        we[y, j:j + 1, :] = wx[1, x * NZ + j]

    def ring_send(t):
        for k, far, hop in ((0, NY // 2, 1), (1, NY - 1 - NY // 2, NY - 1)):
            if t <= far:
                c = lax.rem(y + (NY - hop) * (t - 1), NY)
                p = {"blk_2": lax.rem(y + hop, NY)}
                send(wf.at[c], wf.at[c], 10 + k, p, ysem.at[k, t - 1, 0])
                send(we.at[c], we.at[c], 14 + k, p, ysem.at[k, t - 1, 1])

    def ring_wait(t):
        for k, far, hop in ((0, NY // 2, 1), (1, NY - 1 - NY // 2, NY - 1)):
            if t <= far:
                c = lax.rem(y + (NY - hop) * t, NY)
                await_bytes(wf.at[c], ysem.at[k, t - 1, 0])
                await_bytes(we.at[c], ysem.at[k, t - 1, 1])

    ring_send(1)

    def tile(m):
        await_bytes(wm.at[m, pl.ds(0, nx_in)], xsem.at[m, 0])
        pm = dot_nt(hrows, wm[m].reshape(NM, LP))
        await_bytes(wx.at[m, pl.ds(0, nx_in)], xsem.at[m, 1])
        for j in range(NZX):
            xpad[m, j:j + 1, :] = wx[m, j]
        xe[m, pl.ds(pl.multiple_of(y * NZX, NZX), NZX), :] = xpad[m].astype(BF)
        pe = dot_nt(hrows, xe[m])
        if m:
            for j in range(NY):
                ptx[j, :, :NM] = pm[8 * j:8 * j + 4]
                ptx[j, :, NM:] = pe[8 * j:8 * j + 4]
        else:
            pscr[:NY * 8] = pm
            pscr[NY * 8:2 * NY * 8] = pe
            for r in range(NT):
                psend[r, :, :NM] = pscr[pl.ds(4 + r, NY, stride=8), :]
                psend[r, :, NM:] = pscr[pl.ds(NY * 8 + 4 + r, NY, stride=8), :]

    tile(0)
    for d in range(1, NS):
        sp = lax.rem(s + d, NS)

        @pl.when(sp != 0)
        def _(d=d, sp=sp):
            send(psend.at[sp - 1], irecv.at[s], 6, sect_peers[d - 1])
    tile(1)
    for d in range(1, NS):
        sp = lax.rem(s + d, NS)

        @pl.when(sp == 0)
        def _(d=d):
            send(ptx, trecv.at[s], 7, sect_peers[d - 1])

    m_ = mult[0]
    n_dy = NX * (NS - 1)

    @pl.when(is_txt)
    def _():
        trecv[0] = ptx[...]
        await_bytes(trecv.at[pl.ds(0, NS - 1)], rsem.at[7])
        tsum[...] = jnp.sum(trecv[...], axis=0)
        tfull[y] = tsum[y]
        for d, p in zip(y_far, y_peers):
            send(tsum.at[lax.rem(y + d, NY)], tfull.at[y], 8, p)
        ring_wait(1)
        ring_send(2)
        await_bytes(tfull.at[pl.ds(0, NY - 1)], rsem.at[8])
        for j in range(NY):
            tbuf[:, j * NM:(j + 1) * NM] = tfull[j, :, :NM]
        tbuf[:, NY * NM:] = jnp.sum(tfull[:, :, NM:], axis=0)
        for i, p in enumerate(sect_peers):
            send(tbuf, tbuf, 16 + i, p, rsem.at[9])
        ring_wait(2)
        ring_send(3)
        ring_wait(3)
        ring_send(4)
        await_bytes(dyr, rsem.at[11])
        await_bytes(irecv.at[pl.ds(0, NS - 1)], ssem.at[6])
        await_bytes(tfull.at[pl.ds(0, NY - 1)], ssem.at[8])
        for i in range(NS - 1):
            await_bytes(tbuf, ssem.at[16 + i])

    @pl.when(jnp.logical_not(is_txt))
    def _():
        irecv[s] = psend[s - 1]
        await_bytes(irecv.at[pl.ds(0, NS - 1)], rsem.at[6])
        ifull[y] = jnp.sum(irecv[...], axis=0).astype(BF)
        for p in y_peers:
            send(ifull.at[y], ifull.at[y], 8, p)
        ring_wait(1)
        ring_send(2)
        await_bytes(ifull.at[pl.ds(0, NY - 1)], rsem.at[8])
        fv = ifull[...].astype(F32)
        extra = jnp.sum(fv[:, :, NM:], axis=0)
        unit, _ = unit_rows(jnp.concatenate([fv[j, :, :NM] for j in range(NY)] + [extra], axis=1))
        emb[zx] = unit.astype(BF)
        for p in zx_peers:
            send(emb.at[zx], emb.at[zx], 9, p, rsem.at[10])
        ring_wait(2)
        ring_send(3)
        NI = NZX * 8
        at_img = pos[0:NI]
        for j in range(1, NS - 1):
            at_img = jnp.where(s == j + 1, pos[j * NI:(j + 1) * NI], at_img)
        hit = at_img[None] == NT * blk + iota((4, NI), 0)
        label = jnp.where(hit, 1.0, -1.0)
        await_bytes(tbuf, rsem.at[9])
        t_unit, t_inv = unit_rows(tbuf[...])
        t_emb = t_unit.astype(BF)
        ring_wait(3)
        ring_send(4)
        await_bytes(emb.at[pl.ds(0, NZX - 1)], rsem.at[10])
        ev = emb[...].reshape(NI, NY * NM + NE)
        logits = m_ * dot_nt(t_emb, ev) + off[0]
        coef = -label * jax.nn.sigmoid(-label * logits)
        coef = jnp.where(iota(coef.shape, 0) < NT, coef, 0.0).astype(BF)
        g = m_ * dot_nn(coef, ev)
        gp = (g - t_unit * jnp.sum(t_unit * g, axis=-1, keepdims=True)) * t_inv
        slot = x * (NS - 1) + s - 1
        dyr[slot] = gp.astype(DY)
        for dx in x_far + [0]:
            for ds in range(NS):
                if dx or ds:
                    peer = {"sect": lax.rem(s + ds, NS), "blk_1": lax.rem(x + dx, NX)}
                    send(dyr.at[slot], dyr.at[slot], 13, peer, rsem.at[11])
        await_bytes(dyr.at[pl.ds(0, n_dy - 1)], rsem.at[11])
        await_bytes(ifull.at[pl.ds(0, NY - 1)], ssem.at[8])
        await_bytes(emb.at[pl.ds(0, NZX - 1)], ssem.at[9])
        await_bytes(emit.at[pl.ds(0, NX * NS - 1)], ssem.at[13])
        await_bytes(irecv.at[pl.ds(0, NS - 2)], ssem.at[6])
        await_bytes(ptx, ssem.at[7])

    for j in range(NX):
        v = sum(dyr[(NS - 1) * j + i].astype(F32) for i in range(NS - 1))
        dls[4 * j:4 * j + 4, :] = v
    n_m, per_y = NY * NZ * K8, NZ * K8
    lane = iota((NX * 4, NM), 1)
    halves = []
    for h in range(n_m // NM):
        t = jnp.zeros((NX * 4, NM), F32)
        for i in range(NM // per_y):
            v = dls[:, (h * (NM // per_y) + i) * NM:(h * (NM // per_y) + i + 1) * NM]
            v = pltpu.roll(v, lax.rem(i * per_y - x * per_y + NM, NM), 1)
            t = jnp.where(lax.div(lane, per_y) == i, v, t)
        halves.append(t)
    d_m = jnp.concatenate(halves, axis=1).astype(BF)
    v = dls[:, NY * NM:]
    t = jnp.zeros((NX * 4, NE), F32)
    for j in range(NY):
        r = pltpu.roll(v, lax.rem(j * NZ - j * NZX - x * NZ + 2 * NE, NE), 1)
        t = jnp.where(lax.div(lane, NZ) == j, r, t)
    d_e = t[:, :NY * NZ].astype(BF)
    ring_wait(4)
    for j in range(NY):
        wes[NZ * j:NZ * (j + 1), :] = we[j]
    o = dot_nn(d_m, wf[...].reshape(n_m, LP)) + dot_nn(d_e, wes[...].astype(BF))
    for j in range(NX):
        osend[j] = o[4 * j:4 * j + 4].astype(OT)
    orecv[x] = osend[x]
    for d, p in zip(x_far, x_peers):
        send(osend.at[lax.rem(x + d, NX)], orecv.at[x], 12, p)
    await_bytes(orecv.at[pl.ds(0, NX - 1)], rsem.at[12])
    out[...] = jnp.sum(orecv[...].astype(F32), axis=0)[:NT, :FFQ]

    await_bytes(hrecv.at[pl.ds(0, NS - 1)], ssem.at[0])
    for k, ref in ((1, wm), (2, wx)):
        n_z = 2 * (NZ - 1)
        await_bytes(ref.at[0, pl.ds(0, n_z)], ssem.at[k])
    for k, ref in ((3, wm), (4, wx), (19, wm), (20, wx)):
        await_bytes(ref.at[0, pl.ds(0, nx_in)], ssem.at[k])
    for k, far in ((0, NY // 2), (1, NY - 1 - NY // 2)):
        await_bytes(wf.at[pl.ds(0, far)], ssem.at[10 + k])
        await_bytes(we.at[pl.ds(0, far)], ssem.at[14 + k])
    await_bytes(hall.at[pl.ds(0, NY - 1)], ssem.at[5])
    await_bytes(orecv.at[pl.ds(0, NX - 1)], ssem.at[12])


def on_device(hidden, w_txt, w_img, b_txt, b_img, mult, off, pos):
    NS, NZ, NX, NY = (lax.axis_size(a) for a in SECT_BLK)
    _, rows, FF = hidden.shape
    D = b_txt.shape[0]
    K = w_txt.shape[1]
    NZX = NZ * NX
    NM, NE = NZX * K8, NZX * NY
    FFQ = FF // NS
    LP = (FFQ + 3 + 127) // 128 * 128
    dims = (NS, NZ, NX, NY, FF)
    vm = pltpu.VMEM
    scratch = [
        vm((rows, FF), BF),
        vm((2, K, FF), BF),
        vm((K, LP), F32),
        vm((2, NZX, K8, LP), BF),
        vm((2, NZX, 1, LP), F32),
        vm((2, NZX, LP), F32),
        vm((NS, 4, LP), BF),
        vm((NS, 4, LP), BF),
        vm((NY, 8, LP), BF),
        vm((2, NE, LP), BF),
        vm((2 * NY * 8 + 8, NM), F32),
        vm((NT, NY, NM + NE), F32),
        vm((NY, 4, NM + NE), F32),
        vm((NS, NY, NM + NE), F32),
        vm((NS, NY, 4, NM + NE), F32),
        vm((NY, NY, NM + NE), BF),
        vm((NY, 4, NM + NE), F32),
        vm((NY, 4, NM + NE), F32),
        vm((4, D), F32),
        vm((NZX, 8, D), BF),
        vm((NX * NS, 4, D), DY),
        vm((NX * (NS - 1), 4, D), DY),
        vm((NX * 4, D), F32),
        vm((NX, 4, LP), OT),
        vm((NX, 4, LP), OT),
        vm((NY, NZ * K8, LP), BF),
        vm((NY, NZ, LP), F32),
        vm((NY * NZ, LP), F32),
        vm((D,), F32),
        vm((D,), F32),
        vm(pos.shape, jnp.int32),
        pltpu.SemaphoreType.DMA((6,)),
        pltpu.SemaphoreType.DMA((21,)),
        pltpu.SemaphoreType.DMA((13,)),
        pltpu.SemaphoreType.DMA((2, NZ - 1, 2)),
        pltpu.SemaphoreType.DMA((2, 2)),
        pltpu.SemaphoreType.DMA((2, NY // 2, 2)),
    ]
    any_ = pl.BlockSpec(memory_space=pl.ANY)
    vmem = pl.BlockSpec(memory_space=pltpu.VMEM)
    smem = pl.BlockSpec(memory_space=pltpu.SMEM)
    return pl.pallas_call(
        functools.partial(kernel, dims),
        out_shape=pltpu.VMEM((NT, FFQ), F32),
        in_specs=[any_, any_, any_, any_, any_, smem, smem, any_],
        out_specs=vmem,
        scratch_shapes=scratch,
        compiler_params=pltpu.CompilerParams(collective_id=0, has_side_effects=True),
    )(
        hidden[0], w_txt.T, w_img.T, b_txt, b_img, mult, off, pos
    )


def solution(mesh):
    finer = Mesh(
        mesh.devices.reshape(mesh.shape["sect"], 4, 4, 8), ("sect", "blk_0", "blk_1", "blk_2")
    )
    placed = (P(SECT_BLK, None, None), P(None, BLK), P(None, BLK), P(), P(), P(), P(), P())
    return jax.shard_map(
        on_device, mesh=finer, in_specs=placed, out_specs=P(BLK, "sect"), check_vma=False
    )
```
